128 devices in a mesh: seq: 32 (over y, z, core), head: 2 (over x_hi), rep: 2 (over x_lo).
Axes of the slice: x: 4 (x_hi: 2, x_lo: 2; x = x_hi * 2 + x_lo), y: 4, z: 4, core: 2. Of those that a mesh axis runs over, the one named last changes fastest.
Arguments:
- queries: bfloat16 [2, 65536, 1024], P('rep', 'seq', 'head'), may hold values from -400 to 400
- key_states: bfloat16 [2, 65536, 1024], P('rep', 'seq', 'head'), may hold values from -6 to 6
- value_states: bfloat16 [2, 65536, 1024], P('rep', 'seq', 'head'), may hold values from -6 to 6
- out_grad: bfloat16 [2, 65536, 1024], P('rep', 'seq', 'head'), may hold values from -4 to 4
- key_mixer: bfloat16 [65536, 256], P('seq'), may hold values from -0.0234375 to 0.0234375
- value_mixer: bfloat16 [65536, 256], P('seq'), may hold values from -0.0234375 to 0.0234375
Outputs:
- query_grad: bfloat16 [2, 65536, 1024], P('rep', 'seq', 'head')
- key_grad: bfloat16 [2, 65536, 1024], P('rep', 'seq', 'head')
- value_grad: bfloat16 [2, 65536, 1024], P('rep', 'seq', 'head')
- key_mixer_grad: float32 [65536, 256], P(('seq', 'head', 'rep'))
- value_mixer_grad: float32 [65536, 256], P(('seq', 'head', 'rep'))
The draws below stay inside these ranges and needn't reach their ends.
All inputs are finite; a program needn't handle non-finite values.
Results may differ from the reference program's by a relative error of at most 0.015.
Values may be sent and summed in bfloat16 or wider, within the bound.
No kernel may reach another device: no remote copies, remote signals or barrier semaphores. Data moves between devices by JAX's collectives and lax.ppermute only.
A program may use at most 128 MiB of HBM per device.

```python
import jax
import jax.numpy as jnp
from jax import lax

HEADS = 16
DH = 64
KP = 256
LEN = 65536
BATCH = 2


def draw_queries(key, part):
    base = jnp.clip(jax.random.normal(key, (BATCH, LEN, HEADS * DH), jnp.float32), -4.0, 4.0)
    return base.astype(jnp.bfloat16)


def draw_out_grad(key, part):
    base = jnp.clip(jax.random.normal(jax.random.fold_in(key, 7), (BATCH, LEN, HEADS * DH), jnp.float32), -4.0, 4.0)
    return base.astype(jnp.bfloat16)


def shard_levels(rng, shape, split, smallest, top_value):
    gain, own = 1.0, jax.random.fold_in(rng, 6)
    for axis_at, shards_of in split:
        heights = jnp.exp(jax.random.uniform(jax.random.fold_in(own, axis_at), (shards_of,), jnp.float32, smallest / len(split), top_value / len(split)))
        gain = gain * jnp.repeat(heights, shape[axis_at] // shards_of).reshape([-1 if axis == axis_at else 1 for axis in range(len(shape))])
    return gain


def scatter_about(own_key, extent, deviation, bound, split=(), kind=jnp.bfloat16):
    values = jax.random.normal(own_key, extent, jnp.float32) * deviation
    if len(split) > 0:
        values = shard_levels(own_key, extent, split, -0.22, 0.18) * values
    return jnp.clip(values, min=-bound, max=bound).astype(kind)


def setup_inputs(seed: int = 0) -> dict:
    splits = jax.random.split(jax.random.key(seed), 7)
    queries = draw_queries(jax.random.fold_in(splits[6], 71), 0)
    key_states = scatter_about(splits[1], (BATCH, LEN, HEADS * DH), 1.0, 6.0, ((0, 2), (1, 32), (2, 2)))
    value_states = scatter_about(splits[2], (BATCH, LEN, HEADS * DH), 1.0, 6.0, ((0, 2), (1, 32), (2, 2)))
    out_grad = draw_out_grad(jax.random.fold_in(splits[6], 71), 0)
    key_mixer = scatter_about(splits[4], (LEN, KP), LEN ** -0.5, 0.0234375, ((0, 32),))
    value_mixer = scatter_about(splits[5], (LEN, KP), LEN ** -0.5, 0.0234375, ((0, 32),))
    return dict(queries=queries, key_states=key_states, value_states=value_states, out_grad=out_grad, key_mixer=key_mixer, value_mixer=value_mixer)


def head_pass(carry, items, key_mixer, value_mixer):
    grad_e, grad_f = carry
    qh, kh, vh, gh = items
    scale = 1.0 / (DH ** 0.5)
    proj_k = jnp.dot(key_mixer.T, kh, preferred_element_type=jnp.float32).astype(jnp.bfloat16)
    proj_v = jnp.dot(value_mixer.T, vh, preferred_element_type=jnp.float32).astype(jnp.bfloat16)
    scores = jnp.dot(qh, proj_k.T, preferred_element_type=jnp.float32) * scale
    probs = jax.nn.softmax(scores, axis=-1)
    probs_b = probs.astype(jnp.bfloat16)
    outs = jnp.dot(probs_b, proj_v, preferred_element_type=jnp.float32)
    delta = jnp.sum(gh.astype(jnp.float32) * outs, axis=1, keepdims=True)
    grad_pv = jnp.dot(probs_b.T, gh, preferred_element_type=jnp.float32).astype(jnp.bfloat16)
    grad_p = jnp.dot(gh, proj_v.T, preferred_element_type=jnp.float32)
    grad_s = (probs * (grad_p - delta) * scale).astype(jnp.bfloat16)
    grad_q = jnp.dot(grad_s, proj_k, preferred_element_type=jnp.float32).astype(jnp.bfloat16)
    grad_pk = jnp.dot(grad_s.T, qh, preferred_element_type=jnp.float32).astype(jnp.bfloat16)
    grad_k = jnp.dot(key_mixer, grad_pk, preferred_element_type=jnp.float32).astype(jnp.bfloat16)
    grad_v = jnp.dot(value_mixer, grad_pv, preferred_element_type=jnp.float32).astype(jnp.bfloat16)
    grad_e = grad_e + jnp.dot(kh, grad_pk.T, preferred_element_type=jnp.float32)
    grad_f = grad_f + jnp.dot(vh, grad_pv.T, preferred_element_type=jnp.float32)
    return (grad_e, grad_f), (grad_q, grad_k, grad_v)


def split_heads(array):
    return array.reshape(LEN, HEADS, DH).transpose(1, 0, 2)


def reference(queries, key_states, value_states, out_grad, key_mixer, value_mixer):
    grad_e = jnp.zeros((LEN, KP), jnp.float32)
    grad_f = jnp.zeros((LEN, KP), jnp.float32)
    query_list, key_list, value_list = [], [], []
    for batch in range(BATCH):
        items = (split_heads(queries[batch]), split_heads(key_states[batch]),
                 split_heads(value_states[batch]), split_heads(out_grad[batch]))
        step = lambda c, x: head_pass(c, x, key_mixer, value_mixer)
        (grad_e, grad_f), (grad_q, grad_k, grad_v) = lax.scan(step, (grad_e, grad_f), items)
        query_list.append(grad_q.transpose(1, 0, 2).reshape(LEN, HEADS * DH))
        key_list.append(grad_k.transpose(1, 0, 2).reshape(LEN, HEADS * DH))
        value_list.append(grad_v.transpose(1, 0, 2).reshape(LEN, HEADS * DH))
    return (jnp.stack(query_list), jnp.stack(key_list), jnp.stack(value_list), grad_e, grad_f)
```

```python
import functools

import jax
import jax.numpy as jnp
from jax import lax
from jax.experimental import pallas as pl
from jax.experimental.pallas import tpu as pltpu
from jax.sharding import Mesh
from jax.sharding import PartitionSpec as P

DH = 64
KP = 256
LOG2E = 1.4426950408889634
SEQ = ("seq_0", "seq_1", "seq_2")
SEQ_HEAD_REP = ("seq_0", "seq_1", "seq_2", "head", "rep")
BF = jnp.bfloat16
F32 = jnp.float32
NT = (((1,), (1,)), ((), ()))
TN = (((0,), (0,)), ((), ()))
VM = pl.BlockSpec(memory_space=pltpu.VMEM)
PARAMS = dict(vmem_limit_bytes=56 * 1024 * 1024)


def shape_of(rows, cols, kind):
    return jax.ShapeDtypeStruct((rows, cols), kind)


def cost(flops, moved):
    return pl.CostEstimate(flops=flops, bytes_accessed=moved, transcendentals=0)


def split_by_core(core, both, keep, send):
    half = KP // 2
    for at, total in enumerate(both):
        out = pl.ds(at * half, half)
        keep[out, :] = total[pl.ds(core * half, half), :].astype(keep.dtype)
        send[out, :] = total[pl.ds((1 - core) * half, half), :].astype(send.dtype)


def project_kernel(k_ref, v_ref, e_ref, f_ref, keep, send, sum_k, sum_v):
    step = pl.program_id(0)
    part_k = lax.dot_general(e_ref[...], k_ref[...], TN, preferred_element_type=F32)
    part_v = lax.dot_general(f_ref[...], v_ref[...], TN, preferred_element_type=F32)

    @pl.when(step == 0)
    def _():
        sum_k[...] = part_k
        sum_v[...] = part_v

    @pl.when(step > 0)
    def _():
        sum_k[...] += part_k
        sum_v[...] += part_v

    @pl.when(step == pl.num_programs(0) - 1)
    def _():
        split_by_core(lax.axis_index("seq_2"), (sum_k, sum_v), keep, send)


def project(k, v, e, f):
    tokens, width = k.shape
    rows = 512
    wide = pl.BlockSpec((rows, width), lambda i: (i, 0))
    thin = pl.BlockSpec((rows, KP), lambda i: (i, 0))
    return pl.pallas_call(
        project_kernel,
        grid=(tokens // rows,),
        in_specs=[wide, wide, thin, thin],
        out_specs=[pl.BlockSpec((KP, width), lambda i: (0, 0))] * 2,
        out_shape=[shape_of(KP, width, F32)] * 2,
        scratch_shapes=[pltpu.VMEM((KP, width), F32)] * 2,
        compiler_params=pltpu.CompilerParams(**PARAMS),
        cost_estimate=cost(4 * tokens * width * KP, 6 << 20),
        name="project",
    )(k, v, e, f)


def core_sum_kernel(keep, got, own, send_1, send_2, send_3):
    size = lax.axis_size("seq_0")
    me = lax.axis_index("seq_0")
    rows = KP // 2 // size
    for step, out in enumerate((own, send_1, send_2, send_3)):
        to = lax.rem(me + step, size)
        for at in range(2):
            cut = pl.ds(at * KP // 2 + to * rows, rows)
            total = keep[cut, :] + got[cut, :].astype(F32)
            out[at * rows : (at + 1) * rows, :] = total.astype(out.dtype)


def y_sum_kernel(own, got_1, got_2, got_3, out):
    total = (own[...] + got_2[...].astype(F32)) + (
        got_1[...].astype(F32) + got_3[...].astype(F32)
    )
    out[...] = total.astype(out.dtype)


def z_sum_kernel(own, got_1, got_2, got_3, out):
    total = (own[...].astype(F32) + got_2[...].astype(F32)) + (
        got_1[...].astype(F32) + got_3[...].astype(F32)
    )
    out[...] = total.astype(out.dtype)


def small(kernel, outs, name, *args):
    return pl.pallas_call(
        kernel,
        in_specs=[VM] * len(args),
        out_specs=[VM] * len(outs),
        out_shape=list(outs),
        compiler_params=pltpu.CompilerParams(**PARAMS),
        cost_estimate=cost(1 << 20, 1 << 20),
        name=name,
    )(*args)


def ring(size, step):
    return [(i, (i + step) % size) for i in range(size)]


def shifted(value, axis, step):
    return lax.ppermute(value, axis, ring(lax.axis_size(axis), step))


def total_over_seq(keep, send, wire):
    width = keep.shape[1]
    rows = KP // lax.axis_size("seq_0")
    got = shifted(send, "seq_2", 1)
    own, *sends = small(
        core_sum_kernel,
        [shape_of(rows, width, F32)] + [shape_of(rows, width, wire)] * 3,
        "core_sum",
        keep,
        got,
    )
    got = [shifted(s, "seq_0", i + 1) for i, s in enumerate(sends)]
    (part,) = small(y_sum_kernel, [shape_of(rows, width, wire)], "y_sum", own, *got)
    got = [shifted(part, "seq_1", i + 1) for i in range(3)]
    (piece,) = small(z_sum_kernel, [shape_of(rows, width, BF)], "z_sum", part, *got)
    pieces = [piece] + [shifted(piece, "seq_0", i + 1) for i in range(3)]
    return pieces + [shifted(p, "seq_2", 1) for p in pieces]


def assemble(pieces, first, second):
    size = lax.axis_size("seq_0")
    me = lax.axis_index("seq_0")
    core = lax.axis_index("seq_2")
    rows = KP // 2 // size
    for at, piece in enumerate(pieces):
        of = lax.rem(me + size - at % size, size)
        half = core if at < size else 1 - core
        out = pl.ds(pl.multiple_of(half * (KP // 2) + of * rows, rows), rows)
        first[out, :] = piece[:rows, :]
        second[out, :] = piece[rows:, :]


def attend_kernel(*refs):
    q_ref, g_ref, *pieces = refs[:10]
    dq_ref, keep, send = refs[10:13]
    pk, pv, pk_t, sum_k, sum_v = refs[13:]
    step = pl.program_id(0)
    width = q_ref.shape[1]
    scale = 1.0 / DH**0.5

    @pl.when(step == 0)
    def _():
        assemble(pieces, pk, pv)
        pk_t[...] = pk[...].T
        sum_k[...] = jnp.zeros_like(sum_k)
        sum_v[...] = jnp.zeros_like(sum_v)

    low = lax.broadcasted_iota(jnp.int32, (KP, 2 * DH), 1) < DH

    def pair(j, carry):
        at = pl.multiple_of(j * 2 * DH, 2 * DH)
        cols = pl.ds(at, 2 * DH)
        q = q_ref[:, cols]
        g = g_ref[:, cols]
        pk_pair = pk[:, cols]
        pv_pair = pv[:, cols]
        none = jnp.zeros_like(pk_pair)
        dpk, dpv, dq_t = [], [], []
        for e in range(2):
            mine = low if e == 0 else jnp.logical_not(low)
            s = lax.dot_general(
                jnp.where(mine, pk_pair, none), q, NT, preferred_element_type=F32
            )
            top = jnp.max(s, axis=0, keepdims=True)
            ex = jnp.exp2((s - top) * (scale * LOG2E))
            share = scale / jnp.sum(ex, axis=0, keepdims=True)
            p = ex * share
            pb = p.astype(BF)
            gp = lax.dot_general(
                jnp.where(mine, pv_pair, none), g, NT, preferred_element_type=F32
            )
            delta = jnp.sum(pb.astype(F32) * gp, axis=0, keepdims=True) * (1.0 / scale)
            ds = (p * (gp - delta)).astype(BF)
            dpv.append(jnp.dot(pb, g, preferred_element_type=F32))
            dpk.append(jnp.dot(ds, q, preferred_element_type=F32))
            rows = pl.ds(pl.multiple_of(at + e * DH, DH), DH)
            dq_t.append(jnp.dot(pk_t[rows, :], ds, preferred_element_type=F32))
        sum_k[:, cols] += jnp.where(low, dpk[0], dpk[1])
        sum_v[:, cols] += jnp.where(low, dpv[0], dpv[1])
        dq_ref[:, cols] = jnp.concatenate(dq_t, axis=0).T.astype(BF)
        return carry

    lax.fori_loop(0, width // (2 * DH), pair, 0)

    @pl.when(step == pl.num_programs(0) - 1)
    def _():
        sum_v[...] = sum_v[...] * (1.0 / scale)
        split_by_core(lax.axis_index("seq_2"), (sum_k, sum_v), keep, send)


def attend(q, g, pieces):
    tokens, width = q.shape
    rows = 512
    wide = pl.BlockSpec((rows, width), lambda i: (i, 0))
    still = pl.BlockSpec((KP, width), lambda i: (0, 0))
    return pl.pallas_call(
        attend_kernel,
        grid=(tokens // rows,),
        in_specs=[wide, wide] + [VM] * len(pieces),
        out_specs=[wide, still, still],
        out_shape=[
            shape_of(tokens, width, BF),
            shape_of(KP, width, F32),
            shape_of(KP, width, BF),
        ],
        scratch_shapes=[
            pltpu.VMEM((KP, width), BF),
            pltpu.VMEM((KP, width), BF),
            pltpu.VMEM((width, KP), BF),
            pltpu.VMEM((KP, width), F32),
            pltpu.VMEM((KP, width), F32),
        ],
        compiler_params=pltpu.CompilerParams(**PARAMS),
        cost_estimate=cost(16 * tokens * width * KP, 8 << 20),
        name="attend",
    )(q, g, *pieces)


def mixer_part_kernel(at_ref, k_ref, v_ref, *refs):
    pieces, (out, dpk, dpv) = refs[:-3], refs[-3:]
    assemble(pieces, dpk, dpv)
    out[:, :KP] = lax.dot_general(
        k_ref[...], dpk[...], NT, preferred_element_type=F32
    ).astype(out.dtype)
    out[:, KP:] = lax.dot_general(
        v_ref[...], dpv[...], NT, preferred_element_type=F32
    ).astype(out.dtype)


def mixer_part(at, k, v, pieces, rows, kind):
    width = k.shape[1]
    wide = pl.BlockSpec((rows, width), lambda i, at: (at[0], 0))
    return pl.pallas_call(
        mixer_part_kernel,
        grid_spec=pltpu.PrefetchScalarGridSpec(
            num_scalar_prefetch=1,
            grid=(1,),
            in_specs=[wide, wide] + [VM] * len(pieces),
            out_specs=pl.BlockSpec((rows, 2 * KP), lambda i, at: (0, 0)),
            scratch_shapes=[pltpu.VMEM((KP, width), BF)] * 2,
        ),
        out_shape=shape_of(rows, 2 * KP, kind),
        compiler_params=pltpu.CompilerParams(**PARAMS),
        cost_estimate=cost(4 * rows * width * KP, 2 << 20),
        name="mixer_part",
    )(at, k, v, *pieces)


def input_grads_kernel(e_ref, f_ref, *refs):
    pieces, (dk, dv, dpk, dpv) = refs[:-4], refs[-4:]

    @pl.when(pl.program_id(0) == 0)
    def _():
        assemble(pieces, dpk, dpv)

    dk[...] = jnp.dot(e_ref[...], dpk[...], preferred_element_type=F32).astype(BF)
    dv[...] = jnp.dot(f_ref[...], dpv[...], preferred_element_type=F32).astype(BF)


def input_grads(e, f, pieces):
    tokens, width = e.shape[0], pieces[0].shape[1]
    rows = 512
    wide = pl.BlockSpec((rows, width), lambda i: (i, 0))
    thin = pl.BlockSpec((rows, KP), lambda i: (i, 0))
    return pl.pallas_call(
        input_grads_kernel,
        grid=(tokens // rows,),
        in_specs=[thin, thin] + [VM] * len(pieces),
        out_specs=[wide, wide],
        out_shape=[shape_of(tokens, width, BF)] * 2,
        scratch_shapes=[pltpu.VMEM((KP, width), BF)] * 2,
        compiler_params=pltpu.CompilerParams(**PARAMS),
        cost_estimate=cost(4 * tokens * width * KP, 6 << 20),
        name="input_grads",
    )(e, f, *pieces)


def mixer_sum_kernel(own, got_1, got_2, got_3, de, df):
    total = (own[...] + got_2[...].astype(F32)) + (
        got_1[...].astype(F32) + got_3[...].astype(F32)
    )
    de[...] = total[:, :KP]
    df[...] = total[:, KP:]


def on_device(queries, key_states, value_states, out_grad, key_mixer, value_mixer):
    q, k, v, g = queries[0], key_states[0], value_states[0], out_grad[0]
    tokens, width = q.shape
    across = ("head", "rep")
    keep, send = project(k, v, key_mixer, value_mixer)
    pieces = total_over_seq(keep, send, F32)
    query_grad, keep, send = attend(q, g, pieces)
    pieces = total_over_seq(keep, send, BF)
    me = lax.axis_index(across)
    near = lax.axis_size(across)
    rows = tokens // near
    got = {}
    for step in (2, 1, 3):
        at = lax.rem(me + step, near).reshape(1)
        got[step] = shifted(mixer_part(at, k, v, pieces, rows, BF), across, step)
    own = mixer_part(me.reshape(1), k, v, pieces, rows, F32)
    key_grad, value_grad = input_grads(key_mixer, value_mixer, pieces)
    mixer_e, mixer_f = small(
        mixer_sum_kernel,
        [shape_of(rows, KP, F32)] * 2,
        "mixer_sum",
        own,
        got[1],
        got[2],
        got[3],
    )
    return (query_grad[None], key_grad[None], value_grad[None], mixer_e, mixer_f)


def solution(mesh):
    split = Mesh(
        mesh.devices.reshape(4, 4, 2, mesh.shape["head"], mesh.shape["rep"]),
        ("seq_0", "seq_1", "seq_2", "head", "rep"),
    )
    data = P("rep", SEQ, "head")
    return jax.shard_map(
        on_device,
        mesh=split,
        in_specs=(data, data, data, data, P(SEQ, None), P(SEQ, None)),
        out_specs=(data, data, data, P(SEQ_HEAD_REP, None), P(SEQ_HEAD_REP, None)),
        check_vma=False,
    )
```

```python
import jax
import jax.numpy as jnp
from jax import lax
from jax.experimental import pallas as pl
from jax.experimental.pallas import tpu as pltpu
from jax.sharding import Mesh
from jax.sharding import PartitionSpec as P

DH = 64
KP = 256
LOG2E = 1.4426950408889634
SEQ = ("seq_0", "seq_1", "seq_2")
SEQ_HEAD_REP = ("seq_0", "seq_1", "seq_2", "head", "rep")
BF = jnp.bfloat16
F32 = jnp.float32
NT = (((1,), (1,)), ((), ()))
TN = (((0,), (0,)), ((), ()))
VM = pl.BlockSpec(memory_space=pltpu.VMEM)


def shape_of(rows, cols, kind):
    return jax.ShapeDtypeStruct((rows, cols), kind)


def cost(flops, moved):
    return pl.CostEstimate(flops=flops, bytes_accessed=moved, transcendentals=0)


def split_by_core(core, both, keep, send):
    half = KP // 2
    for at, total in enumerate(both):
        out = pl.ds(at * half, half)
        keep[out, :] = total[pl.ds(core * half, half), :].astype(keep.dtype)
        send[out, :] = total[pl.ds((1 - core) * half, half), :].astype(send.dtype)


def project_kernel(k_ref, v_ref, e_ref, f_ref, keep, send, sum_k, sum_v):
    step = pl.program_id(0)
    part_k = lax.dot_general(e_ref[...], k_ref[...], TN, preferred_element_type=F32)
    part_v = lax.dot_general(f_ref[...], v_ref[...], TN, preferred_element_type=F32)

    @pl.when(step == 0)
    def _():
        sum_k[...] = part_k
        sum_v[...] = part_v

    @pl.when(step > 0)
    def _():
        sum_k[...] += part_k
        sum_v[...] += part_v

    @pl.when(step == pl.num_programs(0) - 1)
    def _():
        split_by_core(lax.axis_index("seq_2"), (sum_k, sum_v), keep, send)


def project(k, v, e, f):
    tokens, width = k.shape
    rows = 512
    wide = pl.BlockSpec((rows, width), lambda i: (i, 0))
    thin = pl.BlockSpec((rows, KP), lambda i: (i, 0))
    return pl.pallas_call(
        project_kernel,
        grid=(tokens // rows,),
        in_specs=[wide, wide, thin, thin],
        out_specs=[pl.BlockSpec((KP, width), lambda i: (0, 0))] * 2,
        out_shape=[shape_of(KP, width, F32)] * 2,
        scratch_shapes=[pltpu.VMEM((KP, width), F32)] * 2,
        compiler_params=pltpu.CompilerParams(vmem_limit_bytes=60 << 20),
        cost_estimate=cost(4 * tokens * width * KP, 6 << 20),
        name="project",
    )(k, v, e, f)


def sum_copies_kernel(got, out):
    total = jnp.sum(got[...].astype(F32), axis=0, keepdims=True)
    out[...] = jnp.broadcast_to(total.astype(out.dtype), out.shape)


def swap(value, axis):
    size = lax.axis_size(axis)
    return lax.ppermute(value, axis, [(i, (i + 1) % size) for i in range(size)])


def total_over_seq(keep, send, wire):
    chips = ("seq_0", "seq_1")
    size = lax.axis_size(chips)
    rows, width = keep.shape
    part = keep + swap(send, "seq_2").astype(F32)
    part = part.astype(wire).reshape(size, rows // size, width)
    got = lax.all_to_all(part, chips, 0, 0, tiled=True)
    copies = pl.pallas_call(
        sum_copies_kernel,
        in_specs=[VM],
        out_specs=VM,
        out_shape=jax.ShapeDtypeStruct(got.shape, BF),
        compiler_params=pltpu.CompilerParams(vmem_limit_bytes=4 << 20),
        cost_estimate=cost(1 << 20, 1 << 20),
        name="sum_copies",
    )(got)
    own = lax.all_to_all(copies, chips, 0, 0, tiled=True).reshape(rows, width)
    return own, swap(own, "seq_2")


def assemble(own, other, first, second):
    half = KP // 2
    core = lax.axis_index("seq_2")
    for piece, at in ((own, core), (other, 1 - core)):
        out = pl.ds(pl.multiple_of(at * half, half), half)
        first[out, :] = piece[:half, :]
        second[out, :] = piece[half:, :]


def attend_kernel(
    q_ref, g_ref, own, other, dq_ref, keep, send, pk, pv, pk_t, sum_k, sum_v
):
    step = pl.program_id(0)
    width = q_ref.shape[1]
    scale = 1.0 / DH**0.5

    @pl.when(step == 0)
    def _():
        assemble(own, other, pk, pv)
        pk_t[...] = pk[...].T
        sum_k[...] = jnp.zeros_like(sum_k)
        sum_v[...] = jnp.zeros_like(sum_v)

    low = lax.broadcasted_iota(jnp.int32, (KP, 2 * DH), 1) < DH

    def pair(j, carry):
        at = pl.multiple_of(j * 2 * DH, 2 * DH)
        cols = pl.ds(at, 2 * DH)
        q = q_ref[:, cols]
        g = g_ref[:, cols]
        pk_pair = pk[:, cols]
        pv_pair = pv[:, cols]
        none = jnp.zeros_like(pk_pair)
        dpk, dpv, dq_t = [], [], []
        for e in range(2):
            mine = low if e == 0 else jnp.logical_not(low)
            s = lax.dot_general(
                jnp.where(mine, pk_pair, none), q, NT, preferred_element_type=F32
            )
            top = jnp.max(s, axis=0, keepdims=True)
            ex = jnp.exp2((s - top) * (scale * LOG2E))
            share = scale / jnp.sum(ex, axis=0, keepdims=True)
            p = ex * share
            pb = p.astype(BF)
            gp = lax.dot_general(
                jnp.where(mine, pv_pair, none), g, NT, preferred_element_type=F32
            )
            delta = jnp.sum(pb.astype(F32) * gp, axis=0, keepdims=True) * (1.0 / scale)
            ds = (p * (gp - delta)).astype(BF)
            dpv.append(jnp.dot(pb, g, preferred_element_type=F32))
            dpk.append(jnp.dot(ds, q, preferred_element_type=F32))
            rows = pl.ds(pl.multiple_of(at + e * DH, DH), DH)
            dq_t.append(jnp.dot(pk_t[rows, :], ds, preferred_element_type=F32))
        sum_k[:, cols] += jnp.where(low, dpk[0], dpk[1])
        sum_v[:, cols] += jnp.where(low, dpv[0], dpv[1])
        dq_ref[:, cols] = jnp.concatenate(dq_t, axis=0).T.astype(BF)
        return carry

    lax.fori_loop(0, width // (2 * DH), pair, 0)

    @pl.when(step == pl.num_programs(0) - 1)
    def _():
        sum_v[...] = sum_v[...] * (1.0 / scale)
        split_by_core(lax.axis_index("seq_2"), (sum_k, sum_v), keep, send)


def attend(q, g, pieces):
    tokens, width = q.shape
    rows = 512
    wide = pl.BlockSpec((rows, width), lambda i: (i, 0))
    still = pl.BlockSpec((KP, width), lambda i: (0, 0))
    return pl.pallas_call(
        attend_kernel,
        grid=(tokens // rows,),
        in_specs=[wide, wide, VM, VM],
        out_specs=[wide, still, still],
        out_shape=[
            shape_of(tokens, width, BF),
            shape_of(KP, width, F32),
            shape_of(KP, width, BF),
        ],
        scratch_shapes=[
            pltpu.VMEM((KP, width), BF),
            pltpu.VMEM((KP, width), BF),
            pltpu.VMEM((width, KP), BF),
            pltpu.VMEM((KP, width), F32),
            pltpu.VMEM((KP, width), F32),
        ],
        compiler_params=pltpu.CompilerParams(vmem_limit_bytes=32 << 20),
        cost_estimate=cost(16 * tokens * width * KP, 8 << 20),
        name="attend",
    )(q, g, *pieces)


def mixer_part_kernel(at_ref, k_ref, v_ref, own, other, out):
    half = KP // 2
    for at, (data, rows) in enumerate(((k_ref, slice(0, half)), (v_ref, slice(half, KP)))):
        for side, piece in enumerate((own, other)):
            cols = slice(at * KP + side * half, at * KP + (side + 1) * half)
            out[:, cols] = lax.dot_general(
                data[...], piece[rows, :], NT, preferred_element_type=F32
            ).astype(out.dtype)


def mixer_part(at, k, v, pieces, rows, kind):
    width = k.shape[1]
    wide = pl.BlockSpec((rows, width), lambda i, at: (at[0], 0))
    return pl.pallas_call(
        mixer_part_kernel,
        grid_spec=pltpu.PrefetchScalarGridSpec(
            num_scalar_prefetch=1,
            grid=(1,),
            in_specs=[wide, wide, VM, VM],
            out_specs=pl.BlockSpec((rows, 2 * KP), lambda i, at: (0, 0)),
        ),
        out_shape=shape_of(rows, 2 * KP, kind),
        compiler_params=pltpu.CompilerParams(vmem_limit_bytes=12 << 20),
        cost_estimate=cost(4 * rows * width * KP, 2 << 20),
        name="mixer_part",
    )(at, k, v, *pieces)


def input_grads_kernel(e_ref, f_ref, own, other, dk, dv, dpk, dpv):
    @pl.when(pl.program_id(0) == 0)
    def _():
        assemble(own, other, dpk, dpv)

    dk[...] = jnp.dot(e_ref[...], dpk[...], preferred_element_type=F32).astype(BF)
    dv[...] = jnp.dot(f_ref[...], dpv[...], preferred_element_type=F32).astype(BF)


def input_grads(e, f, pieces):
    tokens, width = e.shape[0], pieces[0].shape[1]
    rows = 512
    wide = pl.BlockSpec((rows, width), lambda i: (i, 0))
    thin = pl.BlockSpec((rows, KP), lambda i: (i, 0))
    return pl.pallas_call(
        input_grads_kernel,
        grid=(tokens // rows,),
        in_specs=[thin, thin, VM, VM],
        out_specs=[wide, wide],
        out_shape=[shape_of(tokens, width, BF)] * 2,
        scratch_shapes=[pltpu.VMEM((KP, width), BF)] * 2,
        compiler_params=pltpu.CompilerParams(vmem_limit_bytes=16 << 20),
        cost_estimate=cost(4 * tokens * width * KP, 6 << 20),
        name="input_grads",
    )(e, f, *pieces)


def mixer_sum_kernel(own, got_1, got_2, got_3, de, df):
    half = KP // 2
    core = lax.axis_index("seq_2")
    total = (own[...] + got_2[...].astype(F32)) + (
        got_1[...].astype(F32) + got_3[...].astype(F32)
    )
    for out, at in ((de, 0), (df, KP)):
        out[:, pl.ds(pl.multiple_of(core * half, half), half)] = total[:, at : at + half]
        out[:, pl.ds(pl.multiple_of((1 - core) * half, half), half)] = total[
            :, at + half : at + KP
        ]


def mixer_sum(own, got):
    rows = own.shape[0]
    block = 128
    wide = pl.BlockSpec((block, 2 * KP), lambda i: (i, 0))
    thin = pl.BlockSpec((block, KP), lambda i: (i, 0))
    return pl.pallas_call(
        mixer_sum_kernel,
        grid=(rows // block,),
        in_specs=[wide] * 4,
        out_specs=[thin] * 2,
        out_shape=[shape_of(rows, KP, F32)] * 2,
        compiler_params=pltpu.CompilerParams(vmem_limit_bytes=8 << 20),
        cost_estimate=cost(1 << 20, 3 << 20),
        name="mixer_sum",
    )(own, got[1], got[2], got[3])


def ring(size, step):
    return [(i, (i + step) % size) for i in range(size)]


def on_device(queries, key_states, value_states, out_grad, key_mixer, value_mixer):
    q, k, v, g = queries[0], key_states[0], value_states[0], out_grad[0]
    tokens, width = q.shape
    across = ("head", "rep")
    keep, send = project(k, v, key_mixer, value_mixer)
    pieces = total_over_seq(keep, send, F32)
    query_grad, keep, send = attend(q, g, pieces)
    pieces = total_over_seq(keep, send, BF)
    me = lax.axis_index(across)
    near = lax.axis_size(across)
    rows = tokens // near
    got = {}
    for step in (2, 1, 3):
        at = lax.rem(me + step, near).reshape(1)
        got[step] = lax.ppermute(
            mixer_part(at, k, v, pieces, rows, BF), across, ring(near, step)
        )
    own = mixer_part(me.reshape(1), k, v, pieces, rows, F32)
    key_grad, value_grad = input_grads(key_mixer, value_mixer, pieces)
    mixer_e, mixer_f = mixer_sum(own, got)
    return (query_grad[None], key_grad[None], value_grad[None], mixer_e, mixer_f)


def solution(mesh):
    split = Mesh(
        mesh.devices.reshape(4, 4, 2, mesh.shape["head"], mesh.shape["rep"]),
        ("seq_0", "seq_1", "seq_2", "head", "rep"),
    )
    data = P("rep", SEQ, "head")
    return jax.shard_map(
        on_device,
        mesh=split,
        in_specs=(data, data, data, data, P(SEQ, None), P(SEQ, None)),
        out_specs=(data, data, data, P(SEQ_HEAD_REP, None), P(SEQ_HEAD_REP, None)),
        check_vma=False,
    )
```

```python
import functools

import jax
import jax.numpy as jnp
from jax import lax
from jax.experimental import pallas as pl
from jax.experimental.pallas import tpu as pltpu
from jax.sharding import Mesh
from jax.sharding import PartitionSpec as P

DH = 64
KP = 256
LOG2E = 1.4426950408889634
ACROSS = ("head", "rep")
SEQ = ("seq_0", "seq_1", "seq_2")
SEQ_HEAD_REP = ("seq_0", "seq_1", "seq_2", "head", "rep")
BF = jnp.bfloat16
F32 = jnp.float32
NT = (((1,), (1,)), ((), ()))
TN = (((0,), (0,)), ((), ()))
VM = pl.BlockSpec(memory_space=pltpu.VMEM)


def shape_of(rows, cols, kind):
    return jax.ShapeDtypeStruct((rows, cols), kind)


def cost(flops, moved):
    return pl.CostEstimate(flops=flops, bytes_accessed=moved, transcendentals=0)


def project_kernel(k_ref, v_ref, e_ref, f_ref, keep, send, k, v, e, f, both, sem):
    chunks = sem.shape[1]
    rows = k.shape[0] // chunks
    half = KP // 2
    core = lax.axis_index("seq_2")
    refs = ((e_ref, e), (k_ref, k), (f_ref, f), (v_ref, v))
    copies = [
        [
            pltpu.make_async_copy(
                source.at[pl.ds(c * rows, rows), :],
                target.at[pl.ds(c * rows, rows), :],
                sem.at[at, c],
            )
            for at, (source, target) in enumerate(refs)
        ]
        for c in range(chunks)
    ]
    for chunk in copies:
        for copy in chunk:
            copy.start()
    for c, chunk in enumerate(copies):
        cut = slice(c * rows, (c + 1) * rows)
        for at, (mixer, data) in enumerate(((e, k), (f, v))):
            chunk[2 * at].wait()
            chunk[2 * at + 1].wait()
            part = lax.dot_general(
                mixer[cut, :], data[cut, :], TN, preferred_element_type=F32
            )
            if c == 0:
                both[at] = part
            else:
                both[at] += part
    for at in range(2):
        out = slice(at * half, (at + 1) * half)
        keep[out, :] = both[at, pl.ds(pl.multiple_of(core * half, half), half), :]
        send[out, :] = both[at, pl.ds(pl.multiple_of((1 - core) * half, half), half), :]


def project(k, v, e, f):
    tokens, width = k.shape
    hbm = pl.BlockSpec(memory_space=pltpu.MemorySpace.HBM)
    return pl.pallas_call(
        project_kernel,
        in_specs=[hbm] * 4,
        out_specs=[VM] * 2,
        out_shape=[shape_of(KP, width, F32)] * 2,
        scratch_shapes=[
            pltpu.VMEM((tokens, width), BF),
            pltpu.VMEM((tokens, width), BF),
            pltpu.VMEM((tokens, KP), BF),
            pltpu.VMEM((tokens, KP), BF),
            pltpu.VMEM((2, KP, width), F32),
            pltpu.SemaphoreType.DMA((4, 4)),
        ],
        compiler_params=pltpu.CompilerParams(vmem_limit_bytes=58 << 20),
        cost_estimate=cost(4 * tokens * width * KP, 6 << 20),
        name="project",
    )(k, v, e, f)


def sum_copies_kernel(got, out):
    total = jnp.sum(got[...].astype(F32), axis=0, keepdims=True)
    out[...] = jnp.broadcast_to(total.astype(out.dtype), out.shape)


def swap(value, axis):
    size = lax.axis_size(axis)
    return lax.ppermute(value, axis, [(i, (i + 1) % size) for i in range(size)])


def total_over_seq(keep, send, wire):
    chips = ("seq_0", "seq_1")
    size = lax.axis_size(chips)
    rows, width = keep.shape
    part = keep + swap(send, "seq_2").astype(F32)
    part = part.astype(wire).reshape(size, rows // size, width)
    got = lax.all_to_all(part, chips, 0, 0, tiled=True)
    copies = pl.pallas_call(
        sum_copies_kernel,
        in_specs=[VM],
        out_specs=VM,
        out_shape=jax.ShapeDtypeStruct(got.shape, BF),
        compiler_params=pltpu.CompilerParams(vmem_limit_bytes=4 << 20),
        cost_estimate=cost(1 << 20, 1 << 20),
        name="sum_copies",
    )(got)
    own = lax.all_to_all(copies, chips, 0, 0, tiled=True).reshape(rows, width)
    return own, swap(own, "seq_2")


def attend_kernel(q_ref, g_ref, own, other, dq_ref, keep, send, sum_k, sum_v):
    step = pl.program_id(0)
    width = q_ref.shape[1]
    half = KP // 2
    scale = 1.0 / DH**0.5
    heads = 4
    lanes = heads * DH

    @pl.when(step == 0)
    def _():
        sum_k[...] = jnp.zeros_like(sum_k)
        sum_v[...] = jnp.zeros_like(sum_v)

    head_of = lax.broadcasted_iota(jnp.int32, (KP, lanes), 1) // DH

    def stacked(piece):
        none = jnp.zeros_like(piece)
        return jnp.concatenate(
            [jnp.where(head_of == h, piece, none) for h in range(heads)], axis=0
        )

    def diagonal(total):
        out = total[:KP]
        for h in range(1, heads):
            out = jnp.where(head_of == h, total[h * KP : (h + 1) * KP], out)
        return out

    def group(j, carry):
        cols = pl.ds(pl.multiple_of(j * lanes, lanes), lanes)
        q = q_ref[:, cols]
        g = g_ref[:, cols]
        pk = stacked(jnp.concatenate([own[:half, cols], other[:half, cols]], axis=0))
        pv = stacked(jnp.concatenate([own[half:, cols], other[half:, cols]], axis=0))
        s_all = lax.dot_general(pk, q, NT, preferred_element_type=F32)
        gp_all = lax.dot_general(pv, g, NT, preferred_element_type=F32)
        pbs, dss = [], []
        for h in range(heads):
            s = s_all[h * KP : (h + 1) * KP]
            gp = gp_all[h * KP : (h + 1) * KP]
            top = jnp.max(s, axis=0, keepdims=True)
            ex = jnp.exp2((s - top) * (scale * LOG2E))
            share = scale / jnp.sum(ex, axis=0, keepdims=True)
            p = ex * share
            pb = p.astype(BF)
            delta = jnp.sum(pb.astype(F32) * gp, axis=0, keepdims=True) * (1.0 / scale)
            pbs.append(pb)
            dss.append((p * (gp - delta)).astype(BF))
        pb = jnp.concatenate(pbs, axis=0)
        ds = jnp.concatenate(dss, axis=0)
        sum_v[:, cols] += diagonal(jnp.dot(pb, g, preferred_element_type=F32))
        sum_k[:, cols] += diagonal(jnp.dot(ds, q, preferred_element_type=F32))
        dq_ref[:, cols] = lax.dot_general(
            ds, pk, TN, preferred_element_type=F32
        ).astype(BF)
        return carry

    lax.fori_loop(0, width // lanes, group, 0)

    @pl.when(step == pl.num_programs(0) - 1)
    def _():
        keep[:half, :] = sum_k[:half, :]
        keep[half:, :] = sum_v[:half, :] * (1.0 / scale)
        send[:half, :] = sum_k[half:, :].astype(send.dtype)
        send[half:, :] = (sum_v[half:, :] * (1.0 / scale)).astype(send.dtype)


def attend(q, g, pieces):
    tokens, width = q.shape
    rows = 1024
    wide = pl.BlockSpec((rows, width), lambda i: (i, 0))
    still = pl.BlockSpec((KP, width), lambda i: (0, 0))
    return pl.pallas_call(
        attend_kernel,
        grid=(tokens // rows,),
        in_specs=[wide, wide, VM, VM],
        out_specs=[wide, still, still],
        out_shape=[
            shape_of(tokens, width, BF),
            shape_of(KP, width, F32),
            shape_of(KP, width, BF),
        ],
        scratch_shapes=[pltpu.VMEM((KP, width), F32)] * 2,
        compiler_params=pltpu.CompilerParams(vmem_limit_bytes=44 << 20),
        cost_estimate=cost(16 * tokens * width * KP, 8 << 20),
        name="attend",
    )(q, g, *pieces)


def mixer_part_kernel(steps, k_ref, v_ref, own, other, *refs):
    extra, (de, df) = refs[:-2], refs[-2:]
    half = KP // 2
    core = lax.axis_index("seq_2")
    size = lax.axis_size(ACROSS)
    rows = de.shape[0]
    for at, (data, out) in enumerate(((k_ref, de), (v_ref, df))):
        to = lax.rem(lax.axis_index(ACROSS) + steps[at], size)
        block = data[pl.ds(pl.multiple_of(to * rows, rows), rows), :]
        for piece, side in ((own, core), (other, 1 - core)):
            part = lax.dot_general(
                block,
                piece[at * half : (at + 1) * half, :],
                NT,
                preferred_element_type=F32,
            )
            cols = pl.ds(pl.multiple_of(side * half, half), half)
            if extra:
                part += extra[at][:, cols].astype(F32)
            out[:, cols] = part.astype(out.dtype)


def mixer_part(steps, k, v, pieces, kind, *extra):
    tokens, width = k.shape
    rows = tokens // lax.axis_size(ACROSS)
    return pl.pallas_call(
        functools.partial(mixer_part_kernel, steps),
        in_specs=[VM] * (4 + len(extra)),
        out_specs=[VM] * 2,
        out_shape=[shape_of(rows, KP, kind)] * 2,
        compiler_params=pltpu.CompilerParams(vmem_limit_bytes=12 << 20),
        cost_estimate=cost(4 * rows * width * KP, 2 << 20),
        name="mixer_part",
    )(k, v, *pieces, *extra)


def input_grads_kernel(e_ref, f_ref, own, other, dk, dv, dpk, dpv):
    @pl.when(pl.program_id(0) == 0)
    def _():
        half = KP // 2
        core = lax.axis_index("seq_2")
        for piece, at in ((own, core), (other, 1 - core)):
            out = pl.ds(pl.multiple_of(at * half, half), half)
            dpk[out, :] = piece[:half, :]
            dpv[out, :] = piece[half:, :]

    dk[...] = jnp.dot(e_ref[...], dpk[...], preferred_element_type=F32).astype(BF)
    dv[...] = jnp.dot(f_ref[...], dpv[...], preferred_element_type=F32).astype(BF)


def input_grads(e, f, pieces):
    tokens, width = e.shape[0], pieces[0].shape[1]
    rows = 512
    wide = pl.BlockSpec((rows, width), lambda i: (i, 0))
    thin = pl.BlockSpec((rows, KP), lambda i: (i, 0))
    return pl.pallas_call(
        input_grads_kernel,
        grid=(tokens // rows,),
        in_specs=[thin, thin, VM, VM],
        out_specs=[wide, wide],
        out_shape=[shape_of(tokens, width, BF)] * 2,
        scratch_shapes=[pltpu.VMEM((KP, width), BF)] * 2,
        compiler_params=pltpu.CompilerParams(vmem_limit_bytes=16 << 20),
        cost_estimate=cost(4 * tokens * width * KP, 6 << 20),
        name="input_grads",
    )(e, f, *pieces)


def along(value, step):
    size = lax.axis_size(ACROSS)
    pairs = [(i, (i + step) % size) for i in range(size)]
    return lax.ppermute(value, ACROSS, pairs)


def mixer_grads(k, v, pieces):
    far_e, far_f = mixer_part((2, 2), k, v, pieces, BF)
    far_e, far_f = along(far_e, 1), along(far_f, -1)
    down_e, up_f = mixer_part((3, 1), k, v, pieces, BF)
    down_e, up_f = along(down_e, -1), along(up_f, 1)
    own_e, own_f = mixer_part((0, 0), k, v, pieces, F32)
    up_e, down_f = mixer_part((1, 3), k, v, pieces, BF, far_e, far_f)
    up_e, down_f = along(up_e, 1), along(down_f, -1)
    return (
        own_e + (down_e.astype(F32) + up_e.astype(F32)),
        own_f + (down_f.astype(F32) + up_f.astype(F32)),
    )


def on_device(queries, key_states, value_states, out_grad, key_mixer, value_mixer):
    q, g = queries[0], out_grad[0]
    k, v = key_states[0], value_states[0]
    keep, send = project(k, v, key_mixer, value_mixer)
    pieces = total_over_seq(keep, send, F32)
    query_grad, keep, send = attend(q, g, pieces)
    pieces = total_over_seq(keep, send, BF)
    mixer_e, mixer_f = mixer_grads(k, v, pieces)
    key_grad, value_grad = input_grads(key_mixer, value_mixer, pieces)
    return (query_grad[None], key_grad[None], value_grad[None], mixer_e, mixer_f)


def solution(mesh):
    split = Mesh(
        mesh.devices.reshape(4, 4, 2, mesh.shape["head"], mesh.shape["rep"]),
        ("seq_0", "seq_1", "seq_2", "head", "rep"),
    )
    data = P("rep", SEQ, "head")
    return jax.shard_map(
        on_device,
        mesh=split,
        in_specs=(data, data, data, data, P(SEQ, None), P(SEQ, None)),
        out_specs=(data, data, data, P(SEQ_HEAD_REP, None), P(SEQ_HEAD_REP, None)),
        check_vma=False,
    )
```

```python
import functools

import jax
import jax.numpy as jnp
from jax import lax
from jax.experimental import pallas as pl
from jax.experimental.pallas import tpu as pltpu
from jax.sharding import Mesh
from jax.sharding import PartitionSpec as P

DH = 64
KP = 256
PLACES = 4
LOG2E = 1.4426950408889634
ACROSS = ("head", "rep")
SEQ = ("seq_0", "seq_1", "seq_2")
SEQ_HEAD_REP = ("seq_0", "seq_1", "seq_2", "head", "rep")
BF = jnp.bfloat16
F32 = jnp.float32
NT = (((1,), (1,)), ((), ()))
TN = (((0,), (0,)), ((), ()))
VM = pl.BlockSpec(memory_space=pltpu.VMEM)


def shape_of(rows, cols, kind):
    return jax.ShapeDtypeStruct((rows, cols), kind)


def cost(flops, moved):
    return pl.CostEstimate(flops=flops, bytes_accessed=moved, transcendentals=0)


def first_place(core):
    y, z = lax.axis_index("seq_0"), lax.axis_index("seq_1")
    return y + core * (z - y)


def project_kernel(k_ref, v_ref, e_ref, f_ref, keep, send, k, v, e, f, both, sem):
    chunks = sem.shape[1]
    rows = k.shape[0] // chunks
    half = KP // 2
    core = lax.axis_index("seq_2")
    refs = ((e_ref, e), (k_ref, k), (f_ref, f), (v_ref, v))
    copies = [
        [
            pltpu.make_async_copy(
                source.at[pl.ds(c * rows, rows), :],
                target.at[pl.ds(c * rows, rows), :],
                sem.at[at, c],
            )
            for at, (source, target) in enumerate(refs)
        ]
        for c in range(chunks)
    ]
    for chunk in copies:
        for copy in chunk:
            copy.start()
    for c, chunk in enumerate(copies):
        cut = slice(c * rows, (c + 1) * rows)
        for at, (mixer, data) in enumerate(((e, k), (f, v))):
            chunk[2 * at].wait()
            chunk[2 * at + 1].wait()
            part = lax.dot_general(
                mixer[cut, :], data[cut, :], TN, preferred_element_type=F32
            )
            if c == 0:
                both[at] = part
            else:
                both[at] += part
    rows = half // PLACES
    for out, side in ((keep, core), (send, 1 - core)):
        me = first_place(side)
        for place in range(PLACES):
            cut = pl.multiple_of(
                side * half + lax.rem(me + PLACES - place, PLACES) * rows, rows
            )
            for at in range(2):
                to = (2 * place + at) * rows
                out[to : to + rows, :] = both[at, pl.ds(cut, rows), :]


def project(k, v, e, f):
    tokens, width = k.shape
    hbm = pl.BlockSpec(memory_space=pltpu.MemorySpace.HBM)
    return pl.pallas_call(
        project_kernel,
        in_specs=[hbm] * 4,
        out_specs=[VM] * 2,
        out_shape=[shape_of(KP, width, F32)] * 2,
        scratch_shapes=[
            pltpu.VMEM((tokens, width), BF),
            pltpu.VMEM((tokens, width), BF),
            pltpu.VMEM((tokens, KP), BF),
            pltpu.VMEM((tokens, KP), BF),
            pltpu.VMEM((2, KP, width), F32),
            pltpu.SemaphoreType.DMA((4, 4)),
        ],
        compiler_params=pltpu.CompilerParams(vmem_limit_bytes=58 << 20),
        cost_estimate=cost(4 * tokens * width * KP, 6 << 20),
        name="project",
    )(k, v, e, f)


def shifts(step, second):
    pairs = []
    for y in range(PLACES):
        for z in range(PLACES):
            for core in range(2):
                to = (y, (z + step) % PLACES) if second != core else ((y + step) % PLACES, z)
                pairs.append(
                    ((y * PLACES + z) * 2 + core, (to[0] * PLACES + to[1]) * 2 + core)
                )
    return pairs


def from_all(values, second):
    return [
        lax.ppermute(value, SEQ, shifts(step, second))
        for step, value in zip((1, 2, 3), values)
    ]


def summed(own, got):
    one, two, three = (g.astype(F32) for g in got)
    return (own.astype(F32) + two) + (one + three)


def swap(value):
    return lax.ppermute(value, "seq_2", [(0, 1), (1, 0)])


def total_over_seq(keep, send, wire):
    rows = keep.shape[0] // PLACES
    total = keep + swap(send).astype(F32)
    blocks = [total[i * rows : (i + 1) * rows] for i in range(PLACES)]
    got = from_all([blocks[-step].astype(wire) for step in (1, 2, 3)], False)
    part = summed(blocks[0], got).astype(wire)
    piece = summed(part, from_all([part] * 3, True)).astype(BF)
    own = jnp.concatenate([piece] + from_all([piece] * 3, False), axis=0)
    return own, swap(own)


def halves_of(piece, at):
    rows = KP // 2 // PLACES
    return [piece[(2 * i + at) * rows : (2 * i + at + 1) * rows] for i in range(PLACES)]


def attend_kernel(q_ref, g_ref, own, other, dq_ref, keep, send, sum_k, sum_v):
    step = pl.program_id(0)
    width = q_ref.shape[1]
    half = KP // 2
    scale = 1.0 / DH**0.5
    heads = 4
    lanes = heads * DH

    @pl.when(step == 0)
    def _():
        sum_k[...] = jnp.zeros_like(sum_k)
        sum_v[...] = jnp.zeros_like(sum_v)

    head_of = lax.broadcasted_iota(jnp.int32, (KP, lanes), 1) // DH

    def stacked(piece):
        none = jnp.zeros_like(piece)
        return jnp.concatenate(
            [jnp.where(head_of == h, piece, none) for h in range(heads)], axis=0
        )

    def diagonal(total):
        out = total[:KP]
        for h in range(1, heads):
            out = jnp.where(head_of == h, total[h * KP : (h + 1) * KP], out)
        return out

    def group(j, carry):
        cols = pl.ds(pl.multiple_of(j * lanes, lanes), lanes)
        q = q_ref[:, cols]
        g = g_ref[:, cols]
        mine, theirs = own[:, cols], other[:, cols]
        pk, pv = (
            stacked(jnp.concatenate(halves_of(mine, at) + halves_of(theirs, at), axis=0))
            for at in range(2)
        )
        s_all = lax.dot_general(pk, q, NT, preferred_element_type=F32)
        gp_all = lax.dot_general(pv, g, NT, preferred_element_type=F32)
        pbs, dss = [], []
        for h in range(heads):
            s = s_all[h * KP : (h + 1) * KP]
            gp = gp_all[h * KP : (h + 1) * KP]
            top = jnp.max(s, axis=0, keepdims=True)
            ex = jnp.exp2((s - top) * (scale * LOG2E))
            share = scale / jnp.sum(ex, axis=0, keepdims=True)
            p = ex * share
            pb = p.astype(BF)
            delta = jnp.sum(pb.astype(F32) * gp, axis=0, keepdims=True) * (1.0 / scale)
            pbs.append(pb)
            dss.append((p * (gp - delta)).astype(BF))
        pb = jnp.concatenate(pbs, axis=0)
        ds = jnp.concatenate(dss, axis=0)
        sum_v[:, cols] += diagonal(jnp.dot(pb, g, preferred_element_type=F32))
        sum_k[:, cols] += diagonal(jnp.dot(ds, q, preferred_element_type=F32))
        dq_ref[:, cols] = lax.dot_general(
            ds, pk, TN, preferred_element_type=F32
        ).astype(BF)
        return carry

    lax.fori_loop(0, width // lanes, group, 0)

    @pl.when(step == pl.num_programs(0) - 1)
    def _():
        rows = half // PLACES
        for out, side in ((keep, 0), (send, half)):
            for place in range(PLACES):
                cut = slice(side + place * rows, side + (place + 1) * rows)
                to = 2 * place * rows
                out[to : to + rows, :] = sum_k[cut, :].astype(out.dtype)
                out[to + rows : to + 2 * rows, :] = (
                    sum_v[cut, :] * (1.0 / scale)
                ).astype(out.dtype)


def attend(q, g, pieces):
    tokens, width = q.shape
    rows = 1024
    wide = pl.BlockSpec((rows, width), lambda i: (i, 0))
    still = pl.BlockSpec((KP, width), lambda i: (0, 0))
    return pl.pallas_call(
        attend_kernel,
        grid=(tokens // rows,),
        in_specs=[wide, wide, VM, VM],
        out_specs=[wide, still, still],
        out_shape=[
            shape_of(tokens, width, BF),
            shape_of(KP, width, F32),
            shape_of(KP, width, BF),
        ],
        scratch_shapes=[pltpu.VMEM((KP, width), F32)] * 2,
        compiler_params=pltpu.CompilerParams(vmem_limit_bytes=44 << 20),
        cost_estimate=cost(16 * tokens * width * KP, 8 << 20),
        name="attend",
    )(q, g, *pieces)


def unpack_kernel(own, other, dpk, dpv):
    half = KP // 2
    rows = half // PLACES
    core = lax.axis_index("seq_2")
    for piece, side in ((own, core), (other, 1 - core)):
        me = first_place(side)
        for place in range(PLACES):
            cut = pl.multiple_of(
                side * half + lax.rem(me + PLACES - place, PLACES) * rows, rows
            )
            for at, out in enumerate((dpk, dpv)):
                to = (2 * place + at) * rows
                out[pl.ds(cut, rows), :] = piece[to : to + rows, :]


def unpack(own, other):
    return pl.pallas_call(
        unpack_kernel,
        in_specs=[VM] * 2,
        out_specs=[VM] * 2,
        out_shape=[shape_of(*own.shape, BF)] * 2,
        compiler_params=pltpu.CompilerParams(vmem_limit_bytes=4 << 20),
        cost_estimate=cost(1 << 20, 1 << 20),
        name="unpack",
    )(own, other)


def mixer_part_kernel(steps, k_ref, v_ref, dpk, dpv, *refs):
    extra, (de, df) = refs[:-2], refs[-2:]
    size = lax.axis_size(ACROSS)
    rows = de.shape[0]
    for at, (data, grad, out) in enumerate(((k_ref, dpk, de), (v_ref, dpv, df))):
        to = lax.rem(lax.axis_index(ACROSS) + steps[at], size)
        part = lax.dot_general(
            data[pl.ds(pl.multiple_of(to * rows, rows), rows), :],
            grad[...],
            NT,
            preferred_element_type=F32,
        )
        if extra:
            part += extra[at][...].astype(F32)
        out[...] = part.astype(out.dtype)


def mixer_part(steps, k, v, pieces, kind, *extra):
    tokens, width = k.shape
    rows = tokens // lax.axis_size(ACROSS)
    return pl.pallas_call(
        functools.partial(mixer_part_kernel, steps),
        in_specs=[VM] * (4 + len(extra)),
        out_specs=[VM] * 2,
        out_shape=[shape_of(rows, KP, kind)] * 2,
        compiler_params=pltpu.CompilerParams(vmem_limit_bytes=12 << 20),
        cost_estimate=cost(4 * rows * width * KP, 2 << 20),
        name="mixer_part",
    )(k, v, *pieces, *extra)


def input_grads_kernel(e_ref, f_ref, dpk, dpv, dk, dv):
    dk[...] = jnp.dot(e_ref[...], dpk[...], preferred_element_type=F32).astype(BF)
    dv[...] = jnp.dot(f_ref[...], dpv[...], preferred_element_type=F32).astype(BF)


def input_grads(e, f, pieces):
    tokens, width = e.shape[0], pieces[0].shape[1]
    rows = 512
    wide = pl.BlockSpec((rows, width), lambda i: (i, 0))
    thin = pl.BlockSpec((rows, KP), lambda i: (i, 0))
    return pl.pallas_call(
        input_grads_kernel,
        grid=(tokens // rows,),
        in_specs=[thin, thin, VM, VM],
        out_specs=[wide, wide],
        out_shape=[shape_of(tokens, width, BF)] * 2,
        compiler_params=pltpu.CompilerParams(vmem_limit_bytes=16 << 20),
        cost_estimate=cost(4 * tokens * width * KP, 6 << 20),
        name="input_grads",
    )(e, f, *pieces)


def along(value, step):
    size = lax.axis_size(ACROSS)
    pairs = [(i, (i + step) % size) for i in range(size)]
    return lax.ppermute(value, ACROSS, pairs)


def mixer_grads(k, v, pieces):
    far_e, far_f = mixer_part((2, 2), k, v, pieces, BF)
    far_e, far_f = along(far_e, 1), along(far_f, -1)
    down_e, up_f = mixer_part((3, 1), k, v, pieces, BF)
    down_e, up_f = along(down_e, -1), along(up_f, 1)
    own_e, own_f = mixer_part((0, 0), k, v, pieces, F32)
    up_e, down_f = mixer_part((1, 3), k, v, pieces, BF, far_e, far_f)
    up_e, down_f = along(up_e, 1), along(down_f, -1)
    return (
        own_e + (down_e.astype(F32) + up_e.astype(F32)),
        own_f + (down_f.astype(F32) + up_f.astype(F32)),
    )


def on_device(queries, key_states, value_states, out_grad, key_mixer, value_mixer):
    q, g = queries[0], out_grad[0]
    k, v = key_states[0], value_states[0]
    keep, send = project(k, v, key_mixer, value_mixer)
    pieces = total_over_seq(keep, send, F32)
    query_grad, keep, send = attend(q, g, pieces)
    pieces = unpack(*total_over_seq(keep, send, BF))
    mixer_e, mixer_f = mixer_grads(k, v, pieces)
    key_grad, value_grad = input_grads(key_mixer, value_mixer, pieces)
    return (query_grad[None], key_grad[None], value_grad[None], mixer_e, mixer_f)


def solution(mesh):
    split = Mesh(
        mesh.devices.reshape(4, 4, 2, mesh.shape["head"], mesh.shape["rep"]),
        ("seq_0", "seq_1", "seq_2", "head", "rep"),
    )
    data = P("rep", SEQ, "head")
    return jax.shard_map(
        on_device,
        mesh=split,
        in_specs=(data, data, data, data, P(SEQ, None), P(SEQ, None)),
        out_specs=(data, data, data, P(SEQ_HEAD_REP, None), P(SEQ_HEAD_REP, None)),
        check_vma=False,
    )
```

```python
import functools

import jax
import jax.numpy as jnp
from jax import lax
from jax.experimental import pallas as pl
from jax.experimental.pallas import tpu as pltpu
from jax.sharding import Mesh
from jax.sharding import PartitionSpec as P

DH = 64
KP = 256
PLACES = 4
LOG2E = 1.4426950408889634
ACROSS = ("head", "rep")
SEQ = ("seq_0", "seq_1", "seq_2")
SEQ_HEAD_REP = ("seq_0", "seq_1", "seq_2", "head", "rep")
BF = jnp.bfloat16
F32 = jnp.float32
NT = (((1,), (1,)), ((), ()))
TN = (((0,), (0,)), ((), ()))
VM = pl.BlockSpec(memory_space=pltpu.VMEM)


def shape_of(rows, cols, kind):
    return jax.ShapeDtypeStruct((rows, cols), kind)


def cost(flops, moved):
    return pl.CostEstimate(flops=flops, bytes_accessed=moved, transcendentals=0)


def first_place(core):
    y, z = lax.axis_index("seq_0"), lax.axis_index("seq_1")
    return y + core * (z - y)


def project_kernel(k_ref, v_ref, e_ref, f_ref, keep, send, k, v, e, f, both, sem):
    chunks = sem.shape[1]
    rows = k.shape[0] // chunks
    half = KP // 2
    core = lax.axis_index("seq_2")
    refs = ((e_ref, e), (k_ref, k), (f_ref, f), (v_ref, v))
    copies = [
        [
            pltpu.make_async_copy(
                source.at[pl.ds(c * rows, rows), :],
                target.at[pl.ds(c * rows, rows), :],
                sem.at[at, c],
            )
            for at, (source, target) in enumerate(refs)
        ]
        for c in range(chunks)
    ]
    for chunk in copies:
        for copy in chunk:
            copy.start()
    for c, chunk in enumerate(copies):
        cut = slice(c * rows, (c + 1) * rows)
        for at, (mixer, data) in enumerate(((e, k), (f, v))):
            chunk[2 * at].wait()
            chunk[2 * at + 1].wait()
            part = lax.dot_general(
                mixer[cut, :], data[cut, :], TN, preferred_element_type=F32
            )
            if c == 0:
                both[at] = part
            else:
                both[at] += part
    rows = half // PLACES
    for out, side in ((keep, core), (send, 1 - core)):
        me = first_place(side)
        for place in range(PLACES):
            cut = pl.multiple_of(
                side * half + lax.rem(me + PLACES - place, PLACES) * rows, rows
            )
            for at in range(2):
                to = (2 * place + at) * rows
                out[to : to + rows, :] = both[at, pl.ds(cut, rows), :]


def project(k, v, e, f):
    tokens, width = k.shape
    hbm = pl.BlockSpec(memory_space=pltpu.MemorySpace.HBM)
    return pl.pallas_call(
        project_kernel,
        in_specs=[hbm] * 4,
        out_specs=[VM] * 2,
        out_shape=[shape_of(KP, width, F32)] * 2,
        scratch_shapes=[
            pltpu.VMEM((tokens, width), BF),
            pltpu.VMEM((tokens, width), BF),
            pltpu.VMEM((tokens, KP), BF),
            pltpu.VMEM((tokens, KP), BF),
            pltpu.VMEM((2, KP, width), F32),
            pltpu.SemaphoreType.DMA((4, 4)),
        ],
        compiler_params=pltpu.CompilerParams(vmem_limit_bytes=52 << 20),
        cost_estimate=cost(4 * tokens * width * KP, 6 << 20),
        name="project",
    )(k, v, e, f)


def shifts(step, second):
    pairs = []
    for y in range(PLACES):
        for z in range(PLACES):
            for core in range(2):
                to = (y, (z + step) % PLACES) if second != core else ((y + step) % PLACES, z)
                pairs.append(
                    ((y * PLACES + z) * 2 + core, (to[0] * PLACES + to[1]) * 2 + core)
                )
    return pairs


def from_all(values, second):
    got = []
    for step, value in zip((1, 2, 3), values):
        got.append(lax.ppermute(value, SEQ, shifts(step, second)))
    return got


def summed(own, got):
    one, two, three = (g.astype(F32) for g in got)
    return (own.astype(F32) + two) + (one + three)


def swap(value):
    return lax.ppermute(value, "seq_2", [(0, 1), (1, 0)])


def total_over_seq(keep, send, wire):
    rows = keep.shape[0] // PLACES
    total = keep + swap(send).astype(F32)
    blocks = [total[i * rows : (i + 1) * rows] for i in range(PLACES)]
    got = from_all([blocks[-step].astype(wire) for step in (1, 2, 3)], False)
    part = summed(blocks[0], got).astype(wire)
    piece = summed(part, from_all([part] * 3, True)).astype(BF)
    own = jnp.concatenate([piece] + from_all([piece] * 3, False), axis=0)
    return own, swap(own)


def halves_of(piece, at):
    rows = KP // 2 // PLACES
    return [piece[(2 * i + at) * rows : (2 * i + at + 1) * rows] for i in range(PLACES)]


def attend_kernel(q_ref, g_ref, own, other, dq_ref, keep, send, sum_k, sum_v):
    step = pl.program_id(0)
    width = q_ref.shape[1]
    half = KP // 2
    scale = 1.0 / DH**0.5
    heads = 4
    lanes = heads * DH

    @pl.when(step == 0)
    def _():
        sum_k[...] = jnp.zeros_like(sum_k)
        sum_v[...] = jnp.zeros_like(sum_v)

    head_of = lax.broadcasted_iota(jnp.int32, (KP, lanes), 1) // DH

    def stacked(piece):
        none = jnp.zeros_like(piece)
        return jnp.concatenate(
            [jnp.where(head_of == h, piece, none) for h in range(heads)], axis=0
        )

    def diagonal(total):
        out = total[:KP]
        for h in range(1, heads):
            out = jnp.where(head_of == h, total[h * KP : (h + 1) * KP], out)
        return out

    def group(j, carry):
        cols = pl.ds(pl.multiple_of(j * lanes, lanes), lanes)
        q = q_ref[:, cols]
        g = g_ref[:, cols]
        mine, theirs = own[:, cols], other[:, cols]
        pk, pv = (
            stacked(jnp.concatenate(halves_of(mine, at) + halves_of(theirs, at), axis=0))
            for at in range(2)
        )
        s_all = lax.dot_general(pk, q, NT, preferred_element_type=F32)
        gp_all = lax.dot_general(pv, g, NT, preferred_element_type=F32)
        pbs, dss = [], []
        for h in range(heads):
            s = s_all[h * KP : (h + 1) * KP]
            gp = gp_all[h * KP : (h + 1) * KP]
            top = jnp.max(s, axis=0, keepdims=True)
            ex = jnp.exp2((s - top) * (scale * LOG2E))
            share = scale / jnp.sum(ex, axis=0, keepdims=True)
            p = ex * share
            pb = p.astype(BF)
            delta = jnp.sum(pb.astype(F32) * gp, axis=0, keepdims=True) * (1.0 / scale)
            pbs.append(pb)
            dss.append((p * (gp - delta)).astype(BF))
        pb = jnp.concatenate(pbs, axis=0)
        ds = jnp.concatenate(dss, axis=0)
        sum_v[:, cols] += diagonal(jnp.dot(pb, g, preferred_element_type=F32))
        sum_k[:, cols] += diagonal(jnp.dot(ds, q, preferred_element_type=F32))
        dq_ref[:, cols] = lax.dot_general(
            ds, pk, TN, preferred_element_type=F32
        ).astype(BF)
        return carry

    lax.fori_loop(0, width // lanes, group, 0)

    @pl.when(step == pl.num_programs(0) - 1)
    def _():
        rows = half // PLACES
        for out, side in ((keep, 0), (send, half)):
            for place in range(PLACES):
                cut = slice(side + place * rows, side + (place + 1) * rows)
                to = 2 * place * rows
                out[to : to + rows, :] = sum_k[cut, :].astype(out.dtype)
                out[to + rows : to + 2 * rows, :] = (
                    sum_v[cut, :] * (1.0 / scale)
                ).astype(out.dtype)


def attend(q, g, pieces):
    tokens, width = q.shape
    rows = 1024
    wide = pl.BlockSpec((rows, width), lambda i: (i, 0))
    still = pl.BlockSpec((KP, width), lambda i: (0, 0))
    return pl.pallas_call(
        attend_kernel,
        grid=(tokens // rows,),
        in_specs=[wide, wide, VM, VM],
        out_specs=[wide, still, still],
        out_shape=[
            shape_of(tokens, width, BF),
            shape_of(KP, width, F32),
            shape_of(KP, width, BF),
        ],
        scratch_shapes=[pltpu.VMEM((KP, width), F32)] * 2,
        compiler_params=pltpu.CompilerParams(vmem_limit_bytes=44 << 20),
        cost_estimate=cost(16 * tokens * width * KP, 8 << 20),
        name="attend",
    )(q, g, *pieces)


def unpack_kernel(own, other, dpk, dpv):
    half = KP // 2
    rows = half // PLACES
    core = lax.axis_index("seq_2")
    for piece, side in ((own, core), (other, 1 - core)):
        me = first_place(side)
        for place in range(PLACES):
            cut = pl.multiple_of(
                side * half + lax.rem(me + PLACES - place, PLACES) * rows, rows
            )
            for at, out in enumerate((dpk, dpv)):
                to = (2 * place + at) * rows
                out[pl.ds(cut, rows), :] = piece[to : to + rows, :]


def unpack(own, other):
    return pl.pallas_call(
        unpack_kernel,
        in_specs=[VM] * 2,
        out_specs=[VM] * 2,
        out_shape=[shape_of(*own.shape, BF)] * 2,
        compiler_params=pltpu.CompilerParams(vmem_limit_bytes=4 << 20),
        cost_estimate=cost(1 << 20, 1 << 20),
        name="unpack",
    )(own, other)


def mixer_part_kernel(steps, k_ref, v_ref, dpk, dpv, *refs):
    extra, (de, df) = refs[:-2], refs[-2:]
    size = lax.axis_size(ACROSS)
    rows = de.shape[0]
    for at, (data, grad, out) in enumerate(((k_ref, dpk, de), (v_ref, dpv, df))):
        to = lax.rem(lax.axis_index(ACROSS) + steps[at], size)
        part = lax.dot_general(
            data[pl.ds(pl.multiple_of(to * rows, rows), rows), :],
            grad[...],
            NT,
            preferred_element_type=F32,
        )
        if extra:
            part += extra[at][...].astype(F32)
        out[...] = part.astype(out.dtype)


def mixer_part(steps, k, v, pieces, kind, *extra):
    tokens, width = k.shape
    rows = tokens // lax.axis_size(ACROSS)
    return pl.pallas_call(
        functools.partial(mixer_part_kernel, steps),
        in_specs=[VM] * (4 + len(extra)),
        out_specs=[VM] * 2,
        out_shape=[shape_of(rows, KP, kind)] * 2,
        compiler_params=pltpu.CompilerParams(vmem_limit_bytes=12 << 20),
        cost_estimate=cost(4 * rows * width * KP, 2 << 20),
        name="mixer_part",
    )(k, v, *pieces, *extra)


def input_grads_kernel(e_ref, f_ref, dpk, dpv, dk, dv):
    dk[...] = jnp.dot(e_ref[...], dpk[...], preferred_element_type=F32).astype(BF)
    dv[...] = jnp.dot(f_ref[...], dpv[...], preferred_element_type=F32).astype(BF)


def input_grads(e, f, pieces):
    tokens, width = e.shape[0], pieces[0].shape[1]
    rows = 512
    wide = pl.BlockSpec((rows, width), lambda i: (i, 0))
    thin = pl.BlockSpec((rows, KP), lambda i: (i, 0))
    return pl.pallas_call(
        input_grads_kernel,
        grid=(tokens // rows,),
        in_specs=[thin, thin, VM, VM],
        out_specs=[wide, wide],
        out_shape=[shape_of(tokens, width, BF)] * 2,
        compiler_params=pltpu.CompilerParams(vmem_limit_bytes=16 << 20),
        cost_estimate=cost(4 * tokens * width * KP, 6 << 20),
        name="input_grads",
    )(e, f, *pieces)


def along(value, step):
    size = lax.axis_size(ACROSS)
    pairs = [(i, (i + step) % size) for i in range(size)]
    return lax.ppermute(value, ACROSS, pairs)


def mixer_grads(k, v, pieces):
    far_e, far_f = mixer_part((2, 2), k, v, pieces, BF)
    far_e, far_f = along(far_e, 1), along(far_f, -1)
    down_e, up_f = mixer_part((3, 1), k, v, pieces, BF)
    down_e, up_f = along(down_e, -1), along(up_f, 1)
    own_e, own_f = mixer_part((0, 0), k, v, pieces, F32)
    up_e, down_f = mixer_part((1, 3), k, v, pieces, BF, far_e, far_f)
    up_e, down_f = along(up_e, 1), along(down_f, -1)
    return (
        own_e + (down_e.astype(F32) + up_e.astype(F32)),
        own_f + (down_f.astype(F32) + up_f.astype(F32)),
    )


def on_device(queries, key_states, value_states, out_grad, key_mixer, value_mixer):
    q, g = queries[0], out_grad[0]
    k, v = key_states[0], value_states[0]
    keep, send = project(k, v, key_mixer, value_mixer)
    pieces = total_over_seq(keep, send, F32)
    query_grad, keep, send = attend(q, g, pieces)
    pieces = total_over_seq(keep, send, BF)
    pieces = unpack(*pieces)
    mixer_e, mixer_f = mixer_grads(k, v, pieces)
    key_grad, value_grad = input_grads(key_mixer, value_mixer, pieces)
    return (query_grad[None], key_grad[None], value_grad[None], mixer_e, mixer_f)


def solution(mesh):
    split = Mesh(
        mesh.devices.reshape(4, 4, 2, mesh.shape["head"], mesh.shape["rep"]),
        ("seq_0", "seq_1", "seq_2", "head", "rep"),
    )
    data = P("rep", SEQ, "head")
    return jax.shard_map(
        on_device,
        mesh=split,
        in_specs=(data, data, data, data, P(SEQ, None), P(SEQ, None)),
        out_specs=(data, data, data, P(SEQ_HEAD_REP, None), P(SEQ_HEAD_REP, None)),
        check_vma=False,
    )
```

```python
import functools

import jax
import jax.numpy as jnp
from jax import lax
from jax.experimental import pallas as pl
from jax.experimental.pallas import tpu as pltpu
from jax.sharding import Mesh
from jax.sharding import PartitionSpec as P

DH = 64
KP = 256
LOG2E = 1.4426950408889634
ACROSS = ("head", "rep")
SEQ = ("seq_0", "seq_1", "seq_2")
SEQ_HEAD_REP = ("seq_0", "seq_1", "seq_2", "head", "rep")
BF = jnp.bfloat16
F32 = jnp.float32
NT = (((1,), (1,)), ((), ()))
TN = (((0,), (0,)), ((), ()))
VM = pl.BlockSpec(memory_space=pltpu.VMEM)


def shape_of(rows, cols, kind):
    return jax.ShapeDtypeStruct((rows, cols), kind)


def cost(flops, moved):
    return pl.CostEstimate(flops=flops, bytes_accessed=moved, transcendentals=0)


def project_kernel(k_ref, v_ref, e_ref, f_ref, keep, send, k, v, e, f, both, sem):
    chunks = sem.shape[1]
    rows = k.shape[0] // chunks
    half = KP // 2
    core = lax.axis_index("seq_2")
    refs = ((e_ref, e), (k_ref, k), (f_ref, f), (v_ref, v))
    copies = [
        [
            pltpu.make_async_copy(
                source.at[pl.ds(c * rows, rows), :],
                target.at[pl.ds(c * rows, rows), :],
                sem.at[at, c],
            )
            for at, (source, target) in enumerate(refs)
        ]
        for c in range(chunks)
    ]
    for chunk in copies:
        for copy in chunk:
            copy.start()
    for c, chunk in enumerate(copies):
        cut = slice(c * rows, (c + 1) * rows)
        for at, (mixer, data) in enumerate(((e, k), (f, v))):
            chunk[2 * at].wait()
            chunk[2 * at + 1].wait()
            part = lax.dot_general(
                mixer[cut, :], data[cut, :], TN, preferred_element_type=F32
            )
            if c == 0:
                both[at] = part
            else:
                both[at] += part
    for out, side in ((keep, core), (send, 1 - core)):
        cut = pl.ds(pl.multiple_of(side * half, half), half)
        for at in range(2):
            out[at * half : (at + 1) * half, :] = both[at, cut, :]


def project(k, v, e, f):
    tokens, width = k.shape
    hbm = pl.BlockSpec(memory_space=pltpu.MemorySpace.HBM)
    return pl.pallas_call(
        project_kernel,
        in_specs=[hbm] * 4,
        out_specs=[VM] * 2,
        out_shape=[shape_of(KP, width, F32)] * 2,
        scratch_shapes=[
            pltpu.VMEM((tokens, width), BF),
            pltpu.VMEM((tokens, width), BF),
            pltpu.VMEM((tokens, KP), BF),
            pltpu.VMEM((tokens, KP), BF),
            pltpu.VMEM((2, KP, width), F32),
            pltpu.SemaphoreType.DMA((4, 4)),
        ],
        compiler_params=pltpu.CompilerParams(vmem_limit_bytes=52 << 20),
        cost_estimate=cost(4 * tokens * width * KP, 6 << 20),
        name="project",
    )(k, v, e, f)


def sum_copies_kernel(got, out):
    total = jnp.sum(got[...].astype(F32), axis=0, keepdims=True)
    out[...] = jnp.broadcast_to(total.astype(out.dtype), out.shape)


def sum_copies(got):
    return pl.pallas_call(
        sum_copies_kernel,
        in_specs=[VM],
        out_specs=VM,
        out_shape=jax.ShapeDtypeStruct(got.shape, BF),
        compiler_params=pltpu.CompilerParams(vmem_limit_bytes=4 << 20),
        cost_estimate=cost(1 << 20, 1 << 20),
        name="sum_copies",
    )(got)


def swap(value):
    return lax.ppermute(value, "seq_2", [(0, 1), (1, 0)])


def total_over_seq(keep, send, wire):
    chips = ("seq_0", "seq_1")
    size = lax.axis_size(chips)
    rows, width = keep.shape
    part = (keep + swap(send).astype(F32)).astype(wire)
    got = lax.all_to_all(
        part.reshape(size, rows // size, width), chips, 0, 0, tiled=True
    )
    own = lax.all_to_all(sum_copies(got), chips, 0, 0, tiled=True).reshape(rows, width)
    return own, swap(own)


def attend_kernel(q_ref, g_ref, own, other, dq_ref, keep, send, sum_k, sum_v):
    step = pl.program_id(0)
    width = q_ref.shape[1]
    half = KP // 2
    scale = 1.0 / DH**0.5
    heads = 4
    lanes = heads * DH

    @pl.when(step == 0)
    def _():
        sum_k[...] = jnp.zeros_like(sum_k)
        sum_v[...] = jnp.zeros_like(sum_v)

    head_of = lax.broadcasted_iota(jnp.int32, (KP, lanes), 1) // DH

    def stacked(piece):
        none = jnp.zeros_like(piece)
        return jnp.concatenate(
            [jnp.where(head_of == h, piece, none) for h in range(heads)], axis=0
        )

    def diagonal(total):
        out = total[:KP]
        for h in range(1, heads):
            out = jnp.where(head_of == h, total[h * KP : (h + 1) * KP], out)
        return out

    def group(j, carry):
        cols = pl.ds(pl.multiple_of(j * lanes, lanes), lanes)
        q = q_ref[:, cols]
        g = g_ref[:, cols]
        pk = stacked(jnp.concatenate([own[:half, cols], other[:half, cols]], axis=0))
        pv = stacked(jnp.concatenate([own[half:, cols], other[half:, cols]], axis=0))
        s_all = lax.dot_general(pk, q, NT, preferred_element_type=F32)
        gp_all = lax.dot_general(pv, g, NT, preferred_element_type=F32)
        pbs, dss = [], []
        for h in range(heads):
            s = s_all[h * KP : (h + 1) * KP]
            gp = gp_all[h * KP : (h + 1) * KP]
            top = jnp.max(s, axis=0, keepdims=True)
            ex = jnp.exp2((s - top) * (scale * LOG2E))
            share = scale / jnp.sum(ex, axis=0, keepdims=True)
            p = ex * share
            pb = p.astype(BF)
            delta = jnp.sum(pb.astype(F32) * gp, axis=0, keepdims=True) * (1.0 / scale)
            pbs.append(pb)
            dss.append((p * (gp - delta)).astype(BF))
        pb = jnp.concatenate(pbs, axis=0)
        ds = jnp.concatenate(dss, axis=0)
        sum_v[:, cols] += diagonal(jnp.dot(pb, g, preferred_element_type=F32))
        sum_k[:, cols] += diagonal(jnp.dot(ds, q, preferred_element_type=F32))
        dq_ref[:, cols] = lax.dot_general(
            ds, pk, TN, preferred_element_type=F32
        ).astype(BF)
        return carry

    lax.fori_loop(0, width // lanes, group, 0)

    @pl.when(step == pl.num_programs(0) - 1)
    def _():
        keep[:half, :] = sum_k[:half, :]
        keep[half:, :] = sum_v[:half, :] * (1.0 / scale)
        send[:half, :] = sum_k[half:, :].astype(send.dtype)
        send[half:, :] = (sum_v[half:, :] * (1.0 / scale)).astype(send.dtype)


def attend(q, g, pieces):
    tokens, width = q.shape
    rows = 1024
    wide = pl.BlockSpec((rows, width), lambda i: (i, 0))
    still = pl.BlockSpec((KP, width), lambda i: (0, 0))
    return pl.pallas_call(
        attend_kernel,
        grid=(tokens // rows,),
        in_specs=[wide, wide, VM, VM],
        out_specs=[wide, still, still],
        out_shape=[
            shape_of(tokens, width, BF),
            shape_of(KP, width, F32),
            shape_of(KP, width, BF),
        ],
        scratch_shapes=[pltpu.VMEM((KP, width), F32)] * 2,
        compiler_params=pltpu.CompilerParams(vmem_limit_bytes=44 << 20),
        cost_estimate=cost(16 * tokens * width * KP, 8 << 20),
        name="attend",
    )(q, g, *pieces)


def unpack_kernel(own, other, dpk, dpv):
    half = KP // 2
    core = lax.axis_index("seq_2")
    for piece, side in ((own, core), (other, 1 - core)):
        cut = pl.ds(pl.multiple_of(side * half, half), half)
        dpk[cut, :] = piece[:half, :]
        dpv[cut, :] = piece[half:, :]


def unpack(own, other):
    return pl.pallas_call(
        unpack_kernel,
        in_specs=[VM] * 2,
        out_specs=[VM] * 2,
        out_shape=[shape_of(*own.shape, BF)] * 2,
        compiler_params=pltpu.CompilerParams(vmem_limit_bytes=4 << 20),
        cost_estimate=cost(1 << 20, 1 << 20),
        name="unpack",
    )(own, other)


def mixer_part_kernel(steps, k_ref, v_ref, dpk, dpv, *refs):
    extra, (de, df) = refs[:-2], refs[-2:]
    size = lax.axis_size(ACROSS)
    rows = de.shape[0]
    for at, (data, grad, out) in enumerate(((k_ref, dpk, de), (v_ref, dpv, df))):
        to = lax.rem(lax.axis_index(ACROSS) + steps[at], size)
        part = lax.dot_general(
            data[pl.ds(pl.multiple_of(to * rows, rows), rows), :],
            grad[...],
            NT,
            preferred_element_type=F32,
        )
        if extra:
            part += extra[at][...].astype(F32)
        out[...] = part.astype(out.dtype)


def mixer_part(steps, k, v, pieces, kind, *extra):
    tokens, width = k.shape
    rows = tokens // lax.axis_size(ACROSS)
    return pl.pallas_call(
        functools.partial(mixer_part_kernel, steps),
        in_specs=[VM] * (4 + len(extra)),
        out_specs=[VM] * 2,
        out_shape=[shape_of(rows, KP, kind)] * 2,
        compiler_params=pltpu.CompilerParams(vmem_limit_bytes=12 << 20),
        cost_estimate=cost(4 * rows * width * KP, 2 << 20),
        name="mixer_part",
    )(k, v, *pieces, *extra)


def input_grads_kernel(e_ref, f_ref, dpk, dpv, dk, dv):
    dk[...] = jnp.dot(e_ref[...], dpk[...], preferred_element_type=F32).astype(BF)
    dv[...] = jnp.dot(f_ref[...], dpv[...], preferred_element_type=F32).astype(BF)


def input_grads(e, f, pieces):
    tokens, width = e.shape[0], pieces[0].shape[1]
    rows = 512
    wide = pl.BlockSpec((rows, width), lambda i: (i, 0))
    thin = pl.BlockSpec((rows, KP), lambda i: (i, 0))
    return pl.pallas_call(
        input_grads_kernel,
        grid=(tokens // rows,),
        in_specs=[thin, thin, VM, VM],
        out_specs=[wide, wide],
        out_shape=[shape_of(tokens, width, BF)] * 2,
        compiler_params=pltpu.CompilerParams(vmem_limit_bytes=16 << 20),
        cost_estimate=cost(4 * tokens * width * KP, 6 << 20),
        name="input_grads",
    )(e, f, *pieces)


def along(value, step):
    size = lax.axis_size(ACROSS)
    pairs = [(i, (i + step) % size) for i in range(size)]
    return lax.ppermute(value, ACROSS, pairs)


def mixer_grads(k, v, pieces):
    far_e, far_f = mixer_part((2, 2), k, v, pieces, BF)
    far_e, far_f = along(far_e, 1), along(far_f, -1)
    down_e, up_f = mixer_part((3, 1), k, v, pieces, BF)
    down_e, up_f = along(down_e, -1), along(up_f, 1)
    own_e, own_f = mixer_part((0, 0), k, v, pieces, F32)
    up_e, down_f = mixer_part((1, 3), k, v, pieces, BF, far_e, far_f)
    up_e, down_f = along(up_e, 1), along(down_f, -1)
    return (
        own_e + (down_e.astype(F32) + up_e.astype(F32)),
        own_f + (down_f.astype(F32) + up_f.astype(F32)),
    )


def on_device(queries, key_states, value_states, out_grad, key_mixer, value_mixer):
    q, g = queries[0], out_grad[0]
    k, v = key_states[0], value_states[0]
    keep, send = project(k, v, key_mixer, value_mixer)
    pieces = total_over_seq(keep, send, F32)
    query_grad, keep, send = attend(q, g, pieces)
    pieces = unpack(*total_over_seq(keep, send, BF))
    mixer_e, mixer_f = mixer_grads(k, v, pieces)
    key_grad, value_grad = input_grads(key_mixer, value_mixer, pieces)
    return (query_grad[None], key_grad[None], value_grad[None], mixer_e, mixer_f)


def solution(mesh):
    split = Mesh(
        mesh.devices.reshape(4, 4, 2, mesh.shape["head"], mesh.shape["rep"]),
        ("seq_0", "seq_1", "seq_2", "head", "rep"),
    )
    data = P("rep", SEQ, "head")
    return jax.shard_map(
        on_device,
        mesh=split,
        in_specs=(data, data, data, data, P(SEQ, None), P(SEQ, None)),
        out_specs=(data, data, data, P(SEQ_HEAD_REP, None), P(SEQ_HEAD_REP, None)),
        check_vma=False,
    )
```

```python
import functools

import jax
import jax.numpy as jnp
from jax import lax
from jax.experimental import pallas as pl
from jax.experimental.pallas import tpu as pltpu
from jax.sharding import Mesh
from jax.sharding import PartitionSpec as P

DH = 64
KP = 256
LOG2E = 1.4426950408889634
ACROSS = ("head", "rep")
SEQ = ("seq_0", "seq_1", "seq_2")
SEQ_HEAD_REP = ("seq_0", "seq_1", "seq_2", "head", "rep")
BF = jnp.bfloat16
F32 = jnp.float32
NT = (((1,), (1,)), ((), ()))
TN = (((0,), (0,)), ((), ()))
VM = pl.BlockSpec(memory_space=pltpu.VMEM)


def shape_of(rows, cols, kind):
    return jax.ShapeDtypeStruct((rows, cols), kind)


def cost(flops, moved):
    return pl.CostEstimate(flops=flops, bytes_accessed=moved, transcendentals=0)


def project_kernel(k_ref, v_ref, e_ref, f_ref, keep, send, k, v, e, f, both, sem):
    chunks = sem.shape[1]
    rows = k.shape[0] // chunks
    half = KP // 2
    core = lax.axis_index("seq_2")
    refs = ((e_ref, e), (k_ref, k), (f_ref, f), (v_ref, v))
    copies = [
        [
            pltpu.make_async_copy(
                source.at[pl.ds(c * rows, rows), :],
                target.at[pl.ds(c * rows, rows), :],
                sem.at[at, c],
            )
            for at, (source, target) in enumerate(refs)
        ]
        for c in range(chunks)
    ]
    for chunk in copies:
        for copy in chunk:
            copy.start()
    for c, chunk in enumerate(copies):
        cut = slice(c * rows, (c + 1) * rows)
        for at, (mixer, data) in enumerate(((e, k), (f, v))):
            chunk[2 * at].wait()
            chunk[2 * at + 1].wait()
            part = lax.dot_general(
                mixer[cut, :], data[cut, :], TN, preferred_element_type=F32
            )
            if c == 0:
                both[at] = part
            else:
                both[at] += part
    for out, side in ((keep, core), (send, 1 - core)):
        cut = pl.ds(pl.multiple_of(side * half, half), half)
        for at in range(2):
            out[at * half : (at + 1) * half, :] = both[at, cut, :]


def project(k, v, e, f):
    tokens, width = k.shape
    hbm = pl.BlockSpec(memory_space=pltpu.MemorySpace.HBM)
    return pl.pallas_call(
        project_kernel,
        in_specs=[hbm] * 4,
        out_specs=[VM] * 2,
        out_shape=[shape_of(KP, width, F32)] * 2,
        scratch_shapes=[
            pltpu.VMEM((tokens, width), BF),
            pltpu.VMEM((tokens, width), BF),
            pltpu.VMEM((tokens, KP), BF),
            pltpu.VMEM((tokens, KP), BF),
            pltpu.VMEM((2, KP, width), F32),
            pltpu.SemaphoreType.DMA((4, 4)),
        ],
        compiler_params=pltpu.CompilerParams(vmem_limit_bytes=52 << 20),
        cost_estimate=cost(4 * tokens * width * KP, 6 << 20),
        name="project",
    )(k, v, e, f)


def sum_copies_kernel(got, out):
    total = jnp.sum(got[...].astype(F32), axis=0, keepdims=True)
    out[...] = jnp.broadcast_to(total.astype(out.dtype), out.shape)


def sum_copies(got):
    return pl.pallas_call(
        sum_copies_kernel,
        in_specs=[VM],
        out_specs=VM,
        out_shape=jax.ShapeDtypeStruct(got.shape, BF),
        compiler_params=pltpu.CompilerParams(vmem_limit_bytes=4 << 20),
        cost_estimate=cost(1 << 20, 1 << 20),
        name="sum_copies",
    )(got)


def swap(value):
    return lax.ppermute(value, "seq_2", [(0, 1), (1, 0)])


def total_over_seq(keep, send, wire):
    chips = ("seq_0", "seq_1")
    size = lax.axis_size(chips)
    rows, width = keep.shape
    part = (keep + swap(send).astype(F32)).astype(wire)
    got = lax.all_to_all(
        part.reshape(size, rows // size, width), chips, 0, 0, tiled=True
    )
    own = lax.all_to_all(sum_copies(got), chips, 0, 0, tiled=True).reshape(rows, width)
    return own, swap(own)


def attend_kernel(q_ref, g_ref, own, other, dq_ref, keep, send, sum_k, sum_v):
    step = pl.program_id(0)
    width = q_ref.shape[1]
    half = KP // 2
    scale = 1.0 / DH**0.5
    heads = 2
    lanes = heads * DH

    @pl.when(step == 0)
    def _():
        sum_k[...] = jnp.zeros_like(sum_k)
        sum_v[...] = jnp.zeros_like(sum_v)

    head_of = lax.broadcasted_iota(jnp.int32, (KP, lanes), 1) // DH

    def stacked(piece):
        none = jnp.zeros_like(piece)
        return jnp.concatenate(
            [jnp.where(head_of == h, piece, none) for h in range(heads)], axis=0
        )

    def diagonal(total):
        out = total[:KP]
        for h in range(1, heads):
            out = jnp.where(head_of == h, total[h * KP : (h + 1) * KP], out)
        return out

    def group(j):
        cols = slice(j * lanes, (j + 1) * lanes)
        q = q_ref[:, cols]
        g = g_ref[:, cols]
        pk = stacked(jnp.concatenate([own[:half, cols], other[:half, cols]], axis=0))
        pv = stacked(jnp.concatenate([own[half:, cols], other[half:, cols]], axis=0))
        s_all = lax.dot_general(pk, q, NT, preferred_element_type=F32)
        gp_all = lax.dot_general(pv, g, NT, preferred_element_type=F32)
        pbs, dss = [], []
        for h in range(heads):
            s = s_all[h * KP : (h + 1) * KP]
            gp = gp_all[h * KP : (h + 1) * KP]
            top = jnp.max(s, axis=0, keepdims=True)
            ex = jnp.exp2((s - top) * (scale * LOG2E))
            share = scale / jnp.sum(ex, axis=0, keepdims=True)
            p = ex * share
            pb = p.astype(BF)
            delta = jnp.sum(pb.astype(F32) * gp, axis=0, keepdims=True) * (1.0 / scale)
            pbs.append(pb)
            dss.append((p * (gp - delta)).astype(BF))
        pb = jnp.concatenate(pbs, axis=0)
        ds = jnp.concatenate(dss, axis=0)
        sum_v[:, cols] += diagonal(jnp.dot(pb, g, preferred_element_type=F32))
        sum_k[:, cols] += diagonal(jnp.dot(ds, q, preferred_element_type=F32))
        dq_ref[:, cols] = lax.dot_general(
            ds, pk, TN, preferred_element_type=F32
        ).astype(BF)

    for j in range(width // lanes):
        group(j)

    @pl.when(step == pl.num_programs(0) - 1)
    def _():
        keep[:half, :] = sum_k[:half, :]
        keep[half:, :] = sum_v[:half, :] * (1.0 / scale)
        send[:half, :] = sum_k[half:, :].astype(send.dtype)
        send[half:, :] = (sum_v[half:, :] * (1.0 / scale)).astype(send.dtype)


def attend(q, g, pieces):
    tokens, width = q.shape
    rows = 512
    wide = pl.BlockSpec((rows, width), lambda i: (i, 0))
    still = pl.BlockSpec((KP, width), lambda i: (0, 0))
    return pl.pallas_call(
        attend_kernel,
        grid=(tokens // rows,),
        in_specs=[wide, wide, VM, VM],
        out_specs=[wide, still, still],
        out_shape=[
            shape_of(tokens, width, BF),
            shape_of(KP, width, F32),
            shape_of(KP, width, BF),
        ],
        scratch_shapes=[pltpu.VMEM((KP, width), F32)] * 2,
        compiler_params=pltpu.CompilerParams(vmem_limit_bytes=44 << 20),
        cost_estimate=cost(16 * tokens * width * KP, 8 << 20),
        name="attend",
    )(q, g, *pieces)


def unpack_kernel(own, other, dpk, dpv):
    half = KP // 2
    core = lax.axis_index("seq_2")
    for piece, side in ((own, core), (other, 1 - core)):
        cut = pl.ds(pl.multiple_of(side * half, half), half)
        dpk[cut, :] = piece[:half, :]
        dpv[cut, :] = piece[half:, :]


def unpack(own, other):
    return pl.pallas_call(
        unpack_kernel,
        in_specs=[VM] * 2,
        out_specs=[VM] * 2,
        out_shape=[shape_of(*own.shape, BF)] * 2,
        compiler_params=pltpu.CompilerParams(vmem_limit_bytes=4 << 20),
        cost_estimate=cost(1 << 20, 1 << 20),
        name="unpack",
    )(own, other)


def mixer_part_kernel(steps, k_ref, v_ref, dpk, dpv, *refs):
    extra, (de, df) = refs[:-2], refs[-2:]
    size = lax.axis_size(ACROSS)
    rows = de.shape[0]
    for at, (data, grad, out) in enumerate(((k_ref, dpk, de), (v_ref, dpv, df))):
        to = lax.rem(lax.axis_index(ACROSS) + steps[at], size)
        part = lax.dot_general(
            data[pl.ds(pl.multiple_of(to * rows, rows), rows), :],
            grad[...],
            NT,
            preferred_element_type=F32,
        )
        if extra:
            part += extra[at][...].astype(F32)
        out[...] = part.astype(out.dtype)


def mixer_part(steps, k, v, pieces, kind, *extra):
    tokens, width = k.shape
    rows = tokens // lax.axis_size(ACROSS)
    return pl.pallas_call(
        functools.partial(mixer_part_kernel, steps),
        in_specs=[VM] * (4 + len(extra)),
        out_specs=[VM] * 2,
        out_shape=[shape_of(rows, KP, kind)] * 2,
        compiler_params=pltpu.CompilerParams(vmem_limit_bytes=12 << 20),
        cost_estimate=cost(4 * rows * width * KP, 2 << 20),
        name="mixer_part",
    )(k, v, *pieces, *extra)


def input_grads_kernel(e_ref, f_ref, dpk, dpv, dk, dv):
    dk[...] = jnp.dot(e_ref[...], dpk[...], preferred_element_type=F32).astype(BF)
    dv[...] = jnp.dot(f_ref[...], dpv[...], preferred_element_type=F32).astype(BF)


def input_grads(e, f, pieces):
    tokens, width = e.shape[0], pieces[0].shape[1]
    rows = 512
    wide = pl.BlockSpec((rows, width), lambda i: (i, 0))
    thin = pl.BlockSpec((rows, KP), lambda i: (i, 0))
    return pl.pallas_call(
        input_grads_kernel,
        grid=(tokens // rows,),
        in_specs=[thin, thin, VM, VM],
        out_specs=[wide, wide],
        out_shape=[shape_of(tokens, width, BF)] * 2,
        compiler_params=pltpu.CompilerParams(vmem_limit_bytes=16 << 20),
        cost_estimate=cost(4 * tokens * width * KP, 6 << 20),
        name="input_grads",
    )(e, f, *pieces)


def mixer_sum_kernel(own_e, down_e, up_e, own_f, down_f, up_f, de, df):
    for own, down, up, out in ((own_e, down_e, up_e, de), (own_f, down_f, up_f, df)):
        out[...] = own[...] + (down[...].astype(F32) + up[...].astype(F32))


def along(value, step):
    size = lax.axis_size(ACROSS)
    pairs = [(i, (i + step) % size) for i in range(size)]
    return lax.ppermute(value, ACROSS, pairs)


def mixer_grads(k, v, pieces):
    far_e, far_f = mixer_part((2, 2), k, v, pieces, BF)
    far_e, far_f = along(far_e, 1), along(far_f, -1)
    down_e, up_f = mixer_part((3, 1), k, v, pieces, BF)
    down_e, up_f = along(down_e, -1), along(up_f, 1)
    own_e, own_f = mixer_part((0, 0), k, v, pieces, F32)
    up_e, down_f = mixer_part((1, 3), k, v, pieces, BF, far_e, far_f)
    up_e, down_f = along(up_e, 1), along(down_f, -1)
    return pl.pallas_call(
        mixer_sum_kernel,
        in_specs=[VM] * 6,
        out_specs=[VM] * 2,
        out_shape=[shape_of(*own_e.shape, F32)] * 2,
        compiler_params=pltpu.CompilerParams(vmem_limit_bytes=8 << 20),
        cost_estimate=cost(1 << 20, 3 << 20),
        name="mixer_sum",
    )(own_e, down_e, up_e, own_f, down_f, up_f)


def on_device(queries, key_states, value_states, out_grad, key_mixer, value_mixer):
    q, g = queries[0], out_grad[0]
    k, v = key_states[0], value_states[0]
    keep, send = project(k, v, key_mixer, value_mixer)
    pieces = total_over_seq(keep, send, F32)
    query_grad, keep, send = attend(q, g, pieces)
    pieces = unpack(*total_over_seq(keep, send, BF))
    mixer_e, mixer_f = mixer_grads(k, v, pieces)
    key_grad, value_grad = input_grads(key_mixer, value_mixer, pieces)
    return (query_grad[None], key_grad[None], value_grad[None], mixer_e, mixer_f)


def solution(mesh):
    split = Mesh(
        mesh.devices.reshape(4, 4, 2, mesh.shape["head"], mesh.shape["rep"]),
        ("seq_0", "seq_1", "seq_2", "head", "rep"),
    )
    data = P("rep", SEQ, "head")
    return jax.shard_map(
        on_device,
        mesh=split,
        in_specs=(data, data, data, data, P(SEQ, None), P(SEQ, None)),
        out_specs=(data, data, data, P(SEQ_HEAD_REP, None), P(SEQ_HEAD_REP, None)),
        check_vma=False,
    )
```

```python
import functools

import jax
import jax.numpy as jnp
from jax import lax
from jax.experimental import pallas as pl
from jax.experimental.pallas import tpu as pltpu
from jax.sharding import Mesh
from jax.sharding import PartitionSpec as P

DH = 64
KP = 256
LOG2E = 1.4426950408889634
ACROSS = ("head", "rep")
SEQ = ("seq_0", "seq_1", "seq_2")
SEQ_HEAD_REP = ("seq_0", "seq_1", "seq_2", "head", "rep")
BF = jnp.bfloat16
F32 = jnp.float32
NT = (((1,), (1,)), ((), ()))
TN = (((0,), (0,)), ((), ()))
VM = pl.BlockSpec(memory_space=pltpu.VMEM)


def shape_of(rows, cols, kind):
    return jax.ShapeDtypeStruct((rows, cols), kind)


def cost(flops, moved):
    return pl.CostEstimate(flops=flops, bytes_accessed=moved, transcendentals=0)


def project_kernel(k_ref, v_ref, e_ref, f_ref, keep, send, k, v, e, f, both, sem):
    chunks = sem.shape[1]
    rows = k.shape[0] // chunks
    half = KP // 2
    core = lax.axis_index("seq_2")
    refs = ((e_ref, e), (k_ref, k), (f_ref, f), (v_ref, v))
    copies = [
        [
            pltpu.make_async_copy(
                source.at[pl.ds(c * rows, rows), :],
                target.at[pl.ds(c * rows, rows), :],
                sem.at[at, c],
            )
            for at, (source, target) in enumerate(refs)
        ]
        for c in range(chunks)
    ]
    for chunk in copies:
        for copy in chunk:
            copy.start()
    for c, chunk in enumerate(copies):
        cut = slice(c * rows, (c + 1) * rows)
        for at, (mixer, data) in enumerate(((e, k), (f, v))):
            chunk[2 * at].wait()
            chunk[2 * at + 1].wait()
            part = lax.dot_general(
                mixer[cut, :], data[cut, :], TN, preferred_element_type=F32
            )
            if c == 0:
                both[at] = part
            else:
                both[at] += part
    for out, side in ((keep, core), (send, 1 - core)):
        cut = pl.ds(pl.multiple_of(side * half, half), half)
        for at in range(2):
            out[at * half : (at + 1) * half, :] = both[at, cut, :]


def project(k, v, e, f):
    tokens, width = k.shape
    hbm = pl.BlockSpec(memory_space=pltpu.MemorySpace.HBM)
    return pl.pallas_call(
        project_kernel,
        in_specs=[hbm] * 4,
        out_specs=[VM] * 2,
        out_shape=[shape_of(KP, width, F32)] * 2,
        scratch_shapes=[
            pltpu.VMEM((tokens, width), BF),
            pltpu.VMEM((tokens, width), BF),
            pltpu.VMEM((tokens, KP), BF),
            pltpu.VMEM((tokens, KP), BF),
            pltpu.VMEM((2, KP, width), F32),
            pltpu.SemaphoreType.DMA((4, 4)),
        ],
        compiler_params=pltpu.CompilerParams(vmem_limit_bytes=52 << 20),
        cost_estimate=cost(4 * tokens * width * KP, 6 << 20),
        name="project",
    )(k, v, e, f)


def sum_copies_kernel(got, out):
    total = jnp.sum(got[...].astype(F32), axis=0, keepdims=True)
    out[...] = jnp.broadcast_to(total.astype(out.dtype), out.shape)


def sum_copies(got):
    return pl.pallas_call(
        sum_copies_kernel,
        in_specs=[VM],
        out_specs=VM,
        out_shape=jax.ShapeDtypeStruct(got.shape, BF),
        compiler_params=pltpu.CompilerParams(vmem_limit_bytes=4 << 20),
        cost_estimate=cost(1 << 20, 1 << 20),
        name="sum_copies",
    )(got)


def swap(value):
    return lax.ppermute(value, "seq_2", [(0, 1), (1, 0)])


def total_over_seq(keep, send, wire):
    chips = ("seq_0", "seq_1")
    size = lax.axis_size(chips)
    rows, width = keep.shape
    part = (keep + swap(send).astype(F32)).astype(wire)
    got = lax.all_to_all(
        part.reshape(size, rows // size, width), chips, 0, 0, tiled=True
    )
    own = lax.all_to_all(sum_copies(got), chips, 0, 0, tiled=True).reshape(rows, width)
    return own, swap(own)


def attend_kernel(q_ref, g_ref, own, other, dq_ref, keep, send, sum_k, sum_v):
    step = pl.program_id(0)
    width = q_ref.shape[1]
    half = KP // 2
    scale = 1.0 / DH**0.5
    heads = 2
    lanes = heads * DH

    @pl.when(step == 0)
    def _():
        sum_k[...] = jnp.zeros_like(sum_k)
        sum_v[...] = jnp.zeros_like(sum_v)

    head_of = lax.broadcasted_iota(jnp.int32, (KP, lanes), 1) // DH

    def stacked(piece):
        none = jnp.zeros_like(piece)
        return jnp.concatenate(
            [jnp.where(head_of == h, piece, none) for h in range(heads)], axis=0
        )

    def diagonal(total):
        out = total[:KP]
        for h in range(1, heads):
            out = jnp.where(head_of == h, total[h * KP : (h + 1) * KP], out)
        return out

    def group(j):
        cols = slice(j * lanes, (j + 1) * lanes)
        q = q_ref[:, cols]
        g = g_ref[:, cols]
        pk = stacked(jnp.concatenate([own[:half, cols], other[:half, cols]], axis=0))
        pv = stacked(jnp.concatenate([own[half:, cols], other[half:, cols]], axis=0))
        s_all = lax.dot_general(pk, q, NT, preferred_element_type=F32)
        gp_all = lax.dot_general(pv, g, NT, preferred_element_type=F32)
        pbs, dss = [], []
        for h in range(heads):
            s = s_all[h * KP : (h + 1) * KP]
            gp = gp_all[h * KP : (h + 1) * KP]
            top = jnp.max(s, axis=0, keepdims=True)
            ex = jnp.exp2((s - top) * (scale * LOG2E))
            share = scale / jnp.sum(ex, axis=0, keepdims=True)
            p = ex * share
            pb = p.astype(BF)
            delta = jnp.sum(pb.astype(F32) * gp, axis=0, keepdims=True) * (1.0 / scale)
            pbs.append(pb)
            dss.append((p * (gp - delta)).astype(BF))
        pb = jnp.concatenate(pbs, axis=0)
        ds = jnp.concatenate(dss, axis=0)
        sum_v[:, cols] += diagonal(jnp.dot(pb, g, preferred_element_type=F32))
        sum_k[:, cols] += diagonal(jnp.dot(ds, q, preferred_element_type=F32))
        dq_ref[:, cols] = lax.dot_general(
            ds, pk, TN, preferred_element_type=F32
        ).astype(BF)

    for j in range(width // lanes):
        group(j)

    @pl.when(step == pl.num_programs(0) - 1)
    def _():
        keep[:half, :] = sum_k[:half, :]
        keep[half:, :] = sum_v[:half, :] * (1.0 / scale)
        send[:half, :] = sum_k[half:, :].astype(send.dtype)
        send[half:, :] = (sum_v[half:, :] * (1.0 / scale)).astype(send.dtype)


def attend(q, g, pieces):
    tokens, width = q.shape
    rows = 512
    wide = pl.BlockSpec((rows, width), lambda i: (i, 0))
    still = pl.BlockSpec((KP, width), lambda i: (0, 0))
    return pl.pallas_call(
        attend_kernel,
        grid=(tokens // rows,),
        in_specs=[wide, wide, VM, VM],
        out_specs=[wide, still, still],
        out_shape=[
            shape_of(tokens, width, BF),
            shape_of(KP, width, F32),
            shape_of(KP, width, BF),
        ],
        scratch_shapes=[pltpu.VMEM((KP, width), F32)] * 2,
        compiler_params=pltpu.CompilerParams(vmem_limit_bytes=44 << 20),
        cost_estimate=cost(16 * tokens * width * KP, 8 << 20),
        name="attend",
    )(q, g, *pieces)


def unpack_kernel(own, other, dpk, dpv):
    half = KP // 2
    core = lax.axis_index("seq_2")
    for piece, side in ((own, core), (other, 1 - core)):
        cut = pl.ds(pl.multiple_of(side * half, half), half)
        dpk[cut, :] = piece[:half, :]
        dpv[cut, :] = piece[half:, :]


def unpack(own, other):
    return pl.pallas_call(
        unpack_kernel,
        in_specs=[VM] * 2,
        out_specs=[VM] * 2,
        out_shape=[shape_of(*own.shape, BF)] * 2,
        compiler_params=pltpu.CompilerParams(vmem_limit_bytes=4 << 20),
        cost_estimate=cost(1 << 20, 1 << 20),
        name="unpack",
    )(own, other)


def mixer_part_kernel(steps, k_ref, v_ref, dpk, dpv, *refs):
    extra, (de, df) = refs[:-2], refs[-2:]
    size = lax.axis_size(ACROSS)
    rows = de.shape[0]
    for at, (data, grad, out) in enumerate(((k_ref, dpk, de), (v_ref, dpv, df))):
        to = lax.rem(lax.axis_index(ACROSS) + steps[at], size)
        part = lax.dot_general(
            data[pl.ds(pl.multiple_of(to * rows, rows), rows), :],
            grad[...],
            NT,
            preferred_element_type=F32,
        )
        if extra:
            part += extra[at][...].astype(F32)
        out[...] = part.astype(out.dtype)


def mixer_part(steps, k, v, pieces, kind, *extra):
    tokens, width = k.shape
    rows = tokens // lax.axis_size(ACROSS)
    return pl.pallas_call(
        functools.partial(mixer_part_kernel, steps),
        in_specs=[VM] * (4 + len(extra)),
        out_specs=[VM] * 2,
        out_shape=[shape_of(rows, KP, kind)] * 2,
        compiler_params=pltpu.CompilerParams(vmem_limit_bytes=12 << 20),
        cost_estimate=cost(4 * rows * width * KP, 2 << 20),
        name="mixer_part",
    )(k, v, *pieces, *extra)


def input_grads_kernel(e_ref, f_ref, dpk, dpv, dk, dv):
    dk[...] = jnp.dot(e_ref[...], dpk[...], preferred_element_type=F32).astype(BF)
    dv[...] = jnp.dot(f_ref[...], dpv[...], preferred_element_type=F32).astype(BF)


def input_grads(e, f, pieces):
    tokens, width = e.shape[0], pieces[0].shape[1]
    rows = 512
    wide = pl.BlockSpec((rows, width), lambda i: (i, 0))
    thin = pl.BlockSpec((rows, KP), lambda i: (i, 0))
    return pl.pallas_call(
        input_grads_kernel,
        grid=(tokens // rows,),
        in_specs=[thin, thin, VM, VM],
        out_specs=[wide, wide],
        out_shape=[shape_of(tokens, width, BF)] * 2,
        compiler_params=pltpu.CompilerParams(vmem_limit_bytes=16 << 20),
        cost_estimate=cost(4 * tokens * width * KP, 6 << 20),
        name="input_grads",
    )(e, f, *pieces)


def mixer_sum_kernel(own_e, down_e, up_e, own_f, down_f, up_f, de, df, sums, sem):
    rows = own_e.shape[0] // 2
    copies = []
    for at, (own, down, up, out) in enumerate(
        ((own_e, down_e, up_e, de), (own_f, down_f, up_f, df))
    ):
        for part in range(2):
            cut = slice(part * rows, (part + 1) * rows)
            sums[at, cut, :] = own[cut, :] + (
                down[cut, :].astype(F32) + up[cut, :].astype(F32)
            )
            copy = pltpu.make_async_copy(
                sums.at[at, pl.ds(part * rows, rows), :],
                out.at[pl.ds(part * rows, rows), :],
                sem.at[at, part],
            )
            copy.start()
            copies.append(copy)
    for copy in copies:
        copy.wait()


def along(value, step):
    size = lax.axis_size(ACROSS)
    pairs = [(i, (i + step) % size) for i in range(size)]
    return lax.ppermute(value, ACROSS, pairs)


def mixer_grads(k, v, pieces):
    far_e, far_f = mixer_part((2, 2), k, v, pieces, BF)
    far_e, far_f = along(far_e, 1), along(far_f, -1)
    down_e, up_f = mixer_part((3, 1), k, v, pieces, BF)
    down_e, up_f = along(down_e, -1), along(up_f, 1)
    own_e, own_f = mixer_part((0, 0), k, v, pieces, F32)
    up_e, down_f = mixer_part((1, 3), k, v, pieces, BF, far_e, far_f)
    up_e, down_f = along(up_e, 1), along(down_f, -1)
    return pl.pallas_call(
        mixer_sum_kernel,
        in_specs=[VM] * 6,
        out_specs=[pl.BlockSpec(memory_space=pltpu.MemorySpace.HBM)] * 2,
        out_shape=[shape_of(*own_e.shape, F32)] * 2,
        scratch_shapes=[
            pltpu.VMEM((2, *own_e.shape), F32),
            pltpu.SemaphoreType.DMA((2, 2)),
        ],
        compiler_params=pltpu.CompilerParams(vmem_limit_bytes=8 << 20),
        cost_estimate=cost(1 << 20, 3 << 20),
        name="mixer_sum",
    )(own_e, down_e, up_e, own_f, down_f, up_f)


def on_device(queries, key_states, value_states, out_grad, key_mixer, value_mixer):
    q, g = queries[0], out_grad[0]
    k, v = key_states[0], value_states[0]
    keep, send = project(k, v, key_mixer, value_mixer)
    pieces = total_over_seq(keep, send, F32)
    query_grad, keep, send = attend(q, g, pieces)
    pieces = unpack(*total_over_seq(keep, send, BF))
    mixer_e, mixer_f = mixer_grads(k, v, pieces)
    key_grad, value_grad = input_grads(key_mixer, value_mixer, pieces)
    return (query_grad[None], key_grad[None], value_grad[None], mixer_e, mixer_f)


def solution(mesh):
    split = Mesh(
        mesh.devices.reshape(4, 4, 2, mesh.shape["head"], mesh.shape["rep"]),
        ("seq_0", "seq_1", "seq_2", "head", "rep"),
    )
    data = P("rep", SEQ, "head")
    return jax.shard_map(
        on_device,
        mesh=split,
        in_specs=(data, data, data, data, P(SEQ, None), P(SEQ, None)),
        out_specs=(data, data, data, P(SEQ_HEAD_REP, None), P(SEQ_HEAD_REP, None)),
        check_vma=False,
    )
```
